32 devices in a mesh: slab: 16 (over z, y, core), tile: 2 (over x).
Axes of the slice: x: 2, y: 2, z: 4, core: 2. Of those that a mesh axis runs over, the one named last changes fastest.
Arguments:
- positions: float32 [64, 3, 128], P(('slab', 'tile')), may hold values from 0 to 150
- weights: float32 [64, 128], P(('slab', 'tile')), may hold values from -6 to 6
- counts: int32 [64], P(('slab', 'tile')), may hold values from 64 to 128
- pairs: int32 [32, 8, 2], P(('slab', 'tile')), may hold values from 0 to 7, as said below
- pair_count: int32 [32], P(('slab', 'tile')), may hold values from 1 to 8
Outputs:
- harmonics: float32 [64, 360, 128], P(('slab', 'tile'))
- zeta: float32 [64, 6, 100], P(('slab', 'tile'))
The draws below stay inside these ranges and needn't reach their ends.
Inputs may be any that keep to these rules, and one draw needn't show every extreme that they name: pairs[d, p, 0] is below 2. pairs[d, p, 1] = h * 2 * 2 + t2 * 2 + k2 names block k2 of tile t2 in the device's slab (h = 0) or in the slab below it (h = 1, never on the first slab); with h = 0 the named block is never earlier in the slab's order of blocks than the local one. Among the first pair_count entries of all devices, each unordered pair of blocks appears at most once; a block paired with itself is allowed.
All inputs are finite; a program needn't handle non-finite values.
Results may differ from the reference program's by a relative error of at most 0.0003.
Values sent between devices are 32-bit elements; how exact they have to be, the bound alone decides.
No kernel may reach another device: no remote copies, remote signals or barrier semaphores. Data moves between devices by JAX's collectives and lax.ppermute only.
A program may use at most 64 MiB of HBM per device.

```python
import math
import jax
import jax.numpy as jnp
import numpy as np
from jax import lax

NBLK = 2
PTS = 128
LIST = 8
NBIN = 10
NHARM = 36
DEVS = 32
BLOCKS = 64
GSET = 8
N_TILE = 2


def pair_plan(key):
    key_scores = jax.random.fold_in(key, 11)
    key_wants = jax.random.fold_in(key, 12)
    span = N_TILE * NBLK
    total = NBLK * GSET
    device = jnp.arange(DEVS, dtype=jnp.int32)
    slab_of = device // N_TILE
    tile_of = device % N_TILE
    candidate = jnp.arange(total, dtype=jnp.int32)
    local = candidate // GSET
    target = candidate % GSET
    half = target // span
    rest = target % span
    lower_ok = (half[None, :] == 1) & (slab_of[:, None] >= 1)
    same_ok = (half[None, :] == 0) & (rest[None, :] >= tile_of[:, None] * NBLK + local[None, :])
    valid = (lower_ok | same_ok).astype(jnp.int32)
    scores = jax.random.randint(key_scores, (DEVS, total), 0, total) * total + candidate[None, :]
    scores = scores + valid * total * total
    _, chosen = lax.top_k(scores, LIST)
    pairs = jnp.stack([local[chosen], target[chosen]], axis=-1).astype(jnp.int32)
    draws = jax.random.randint(key_wants, (DEVS,), 0, LIST + 1)
    wants = jnp.maximum(1, LIST // 4 + draws * draws // (2 * LIST))
    wants = wants.at[0].set(1)
    wants = wants.at[N_TILE].set(LIST)
    count = jnp.minimum(wants, jnp.sum(valid, axis=1)).astype(jnp.int32)
    return (pairs, count)


def draw_pairs(key, part):
    return pair_plan(key)[0]


def draw_pair_count(key, part):
    return pair_plan(key)[1]


def draw_counts(key, part):
    values = jax.random.randint(jax.random.fold_in(key, 21), (BLOCKS,), PTS // 2, PTS + 1)
    values = values.at[0].set(PTS)
    values = values.at[1].set(PTS // 2)
    return values.astype(jnp.int32)


def steps_of(key, dims, cuts, smallest, largest):
    factor_of, own = 1.0, jax.random.fold_in(key, 6)
    for position, blocks in cuts:
        heights = jnp.exp(jax.random.uniform(jax.random.fold_in(own, position), (blocks,), jnp.float32, smallest / len(cuts), largest / len(cuts)))
        factor_of = factor_of * jnp.repeat(heights, dims[position] // blocks).reshape([-1 if axis == position else 1 for axis in range(len(dims))])
    return factor_of


def noise(stream_key, shape, spread, most, shards=(), kind=jnp.bfloat16):
    gain = steps_of(stream_key, shape, shards, -0.22, 0.18) if shards else 1.0
    values = jax.random.normal(stream_key, shape, jnp.float32) * spread * gain
    return jnp.minimum(jnp.maximum(values, -most), most).astype(kind)


def setup_inputs(seed: int = 0) -> dict:
    keys = jax.random.split(jax.random.key(seed), 6)
    positions = jnp.clip(150.0 * jax.random.uniform(keys[0], (BLOCKS, 3, PTS), jnp.float32) ** steps_of(keys[0], (BLOCKS, 3, PTS), ((0, 32),), -0.2, 0.2), 0.0, 150.0)
    weights = noise(keys[1], (BLOCKS, PTS), 1.0, 6.0, ((0, 32),), jnp.float32)
    counts = draw_counts(jax.random.fold_in(keys[5], 71), 0)
    pairs = draw_pairs(jax.random.fold_in(keys[5], 71), 0)
    pair_count = draw_pair_count(jax.random.fold_in(keys[5], 71), 0)
    return dict(positions=positions, weights=weights, counts=counts, pairs=pairs, pair_count=pair_count)


HIGH = lax.Precision.HIGHEST
reach = 150.0

def solid_harmonics(unit_x, unit_y, unit_z):
    unity = jnp.ones_like(unit_z)
    cosine_parts = [unity]
    sine_parts = [jnp.zeros_like(unit_z)]
    for azimuth in range(1, 6):
        cosine_prev = cosine_parts[-1]
        sine_prev = sine_parts[-1]
        cosine_parts.append(cosine_prev * unit_x - sine_prev * unit_y)
        sine_parts.append(sine_prev * unit_x + cosine_prev * unit_y)
    legendre = {}
    for azimuth in range(6):
        diagonal = float(math.prod(range(2 * azimuth - 1, 0, -2)))
        legendre[azimuth, azimuth] = diagonal * unity
        if azimuth + 1 <= 5:
            legendre[azimuth + 1, azimuth] = (2 * azimuth + 1) * diagonal * unit_z
        for degree in range(azimuth + 2, 6):
            legendre[degree, azimuth] = ((2 * degree - 1) * unit_z * legendre[degree - 1, azimuth] - (degree + azimuth - 1) * legendre[degree - 2, azimuth]) / (degree - azimuth)
    result = []
    for degree in range(6):
        for signed in range(-degree, degree + 1):
            azimuth = abs(signed)
            factor = math.sqrt((2 * degree + 1) / (4 * math.pi) * math.factorial(degree - azimuth) / math.factorial(degree + azimuth))
            if azimuth > 0:
                factor = factor * math.sqrt(2.0)
            trig = sine_parts[azimuth] if signed < 0 else cosine_parts[azimuth]
            result.append(factor * legendre[degree, azimuth] * trig)
    return jnp.stack(result)

def parity_table():
    return np.array([(-1.0) ** degree for degree in range(6) for _ in range(2 * degree + 1)], dtype=np.float32)

def pair_terms(first_pos, second_pos, first_live, second_live):
    offset = second_pos[:, None, :] - first_pos[:, :, None]
    distance = jnp.sqrt(lax.optimization_barrier(jnp.sum(offset * offset, axis=0)))
    inverse = 1.0 / jnp.maximum(distance, 1.0)
    harm = solid_harmonics(offset[0] * inverse, offset[1] * inverse, offset[2] * inverse)
    spacing = reach / (NBIN + 1)
    centres = (jnp.arange(NBIN, dtype=jnp.float32) + 1.0) * spacing
    radial = jnp.maximum(0.0, 1.0 - jnp.abs(distance[None] - centres[:, None, None]) / spacing)
    forward = jnp.einsum('kij,bij->kbi', harm, radial * second_live[None, None, :], precision=HIGH)
    flipped = jnp.einsum('kij,bij->kbj', harm, radial * first_live[None, :, None], precision=HIGH)
    flipped = flipped * jnp.asarray(parity_table())[:, None, None]
    return (forward.reshape(NHARM * NBIN, -1), flipped.reshape(NHARM * NBIN, -1))

def block_zeta(harm_block, live):
    shaped = harm_block.reshape(harm_block.shape[0], NHARM, NBIN, harm_block.shape[-1])
    levels = []
    for degree in range(6):
        piece = shaped[:, degree * degree:(degree + 1) * (degree + 1)]
        value = jnp.einsum('zkxi,zkyi->zxy', piece * live[:, None, None, :], piece, precision=HIGH) / PTS
        levels.append(value.reshape(value.shape[0], NBIN * NBIN))
    return jnp.stack(levels, axis=1)

def reference(positions, weights, counts, pairs, pair_count):
    slot = jnp.arange(PTS, dtype=jnp.int32)
    live = weights * (slot[None, :] < counts[:, None]).astype(jnp.float32)
    span = N_TILE * NBLK
    dev_ids = jnp.repeat(jnp.arange(DEVS, dtype=jnp.int32), LIST)
    local = pairs[:, :, 0].reshape(-1).astype(jnp.int32)
    target = pairs[:, :, 1].reshape(-1).astype(jnp.int32)
    active = (jnp.arange(LIST, dtype=jnp.int32)[None, :] < pair_count[:, None]).reshape(-1)
    half = target // span
    rest = target % span
    first = dev_ids * NBLK + local
    second = jnp.where(active, (dev_ids // N_TILE - half) * span + rest, first).astype(jnp.int32)
    accum = jnp.zeros((BLOCKS, NHARM * NBIN, PTS), jnp.float32)

    def step(accum, item):
        first_idx, second_idx, flag = item

        def work(accum):
            first_pos = lax.dynamic_index_in_dim(positions, first_idx, 0, keepdims=False)
            second_pos = lax.dynamic_index_in_dim(positions, second_idx, 0, keepdims=False)
            first_live = lax.dynamic_index_in_dim(live, first_idx, 0, keepdims=False)
            second_live = lax.dynamic_index_in_dim(live, second_idx, 0, keepdims=False)
            forward, flipped = pair_terms(first_pos, second_pos, first_live, second_live)
            row = lax.dynamic_index_in_dim(accum, first_idx, 0, keepdims=False)
            accum = lax.dynamic_update_index_in_dim(accum, row + forward, first_idx, 0)
            other = jnp.where(first_idx == second_idx, 0.0, 1.0).astype(jnp.float32)
            row = lax.dynamic_index_in_dim(accum, second_idx, 0, keepdims=False)
            return lax.dynamic_update_index_in_dim(accum, row + other * flipped, second_idx, 0)
        return (lax.cond(flag, work, lambda value: value, accum), None)
    accum, _ = lax.scan(step, accum, (first, second, active))
    return (accum, block_zeta(accum, live))
```

```python
import math

import jax
import jax.numpy as jnp
from jax import lax
from jax.experimental import pallas as pl
from jax.experimental.pallas import tpu as pltpu
from jax.sharding import PartitionSpec as P

NBIN = 10
DEGREES = 6
NHARM = DEGREES * DEGREES
BPAD = 16
SPACING = 150.0 / (NBIN + 1)
SUB = 8
STEP = 2
HIGH = lax.Precision.HIGHEST


def harmonic_scales():
    out = []
    for l in range(DEGREES):
        for signed in range(-l, l + 1):
            m = abs(signed)
            norm = math.sqrt((2 * l + 1) / (4 * math.pi) * math.factorial(l - m) / math.factorial(l + m))
            if m > 0:
                norm *= math.sqrt(2.0)
            lead = math.prod(range(2 * l - 1, 0, -2)) / math.factorial(l - m)
            out.append(norm * lead)
    return out


def harmonics_of(x, y, z, w):
    s = z * z
    q = {
        (2, 0): s - 1.0 / 3.0,
        (3, 1): s - 0.2,
        (4, 2): s - 1.0 / 7.0,
        (5, 3): s - 1.0 / 9.0,
        (3, 0): z * (s - 0.6),
        (4, 1): z * (s - 3.0 / 7.0),
        (4, 0): s * (s - 6.0 / 7.0) + 3.0 / 35.0,
        (5, 1): s * (s - 2.0 / 3.0) + 1.0 / 21.0,
        (5, 0): z * (s * (s - 10.0 / 9.0) + 5.0 / 21.0),
    }
    q[5, 2] = z * q[2, 0]
    for m in range(DEGREES - 1):
        q[m + 1, m] = z
    cosine, sine = [w], [None]
    for m in range(1, DEGREES):
        if m == 1:
            cosine.append(w * x)
            sine.append(w * y)
        else:
            cosine.append(cosine[-1] * x - sine[-1] * y)
            sine.append(sine[-1] * x + cosine[-2] * y)
    out = []
    for l in range(DEGREES):
        for signed in range(-l, l + 1):
            m = abs(signed)
            trig = sine[m] if signed < 0 else cosine[m]
            out.append(trig if l == m else q[l, m] * trig)
    return out


def kernel(tiles, nblk, rows_dev, lists, place, own_m, one_m, two_m, own_v, one_v, two_v, harm, zeta, data, edges, tally, cols, ybuf, rbuf, acc, hbuf):
    span = tiles * nblk
    part = tiles * rows_dev
    base_meta = nblk * 4
    me = place[0]
    slab_parity = place[1]
    below = jnp.where(slab_parity == 0, 2, 1)
    above = 3 - below

    data[0:part, :] = own_v[...]
    data[part : 2 * part, :] = one_v[...]
    data[2 * part : 3 * part, :] = two_v[...]

    def seat(t):
        return jnp.bitwise_xor(t, me) if tiles == 2 else t

    for k in range(nblk):
        tally[k] = 0

    def add_edge(mine, array, t, blk):
        n = tally[mine]
        edges[mine, n] = array * part + seat(t) * rows_dev + blk * 4
        tally[mine] = n + 1

    def entry(meta, t, p):
        row = seat(t) * rows_dev + base_meta
        a = meta[row, 2 * p].astype(jnp.int32)
        b = meta[row, 2 * p + 1].astype(jnp.int32)
        h = b // span
        rem = b - h * span
        return a, h, rem // nblk, rem % nblk

    def length(meta, t):
        return meta[seat(t) * rows_dev + base_meta, 2 * lists].astype(jnp.int32)

    def own_list(p, c):
        a, h, t2, k2 = entry(own_m, me, p)
        add_edge(a, jnp.where(h == 0, 0, below), t2, k2)

        @pl.when((h == 0) & (t2 == me) & (k2 != a))
        def _():
            add_edge(k2, 0, me, a)

        return c

    lax.fori_loop(0, length(own_m, me), own_list, 0)

    def slab_list(meta, array, half, t):
        def body(p, c):
            a, h, t2, k2 = entry(meta, t, p)

            @pl.when((h == half) & (t2 == me))
            def _():
                add_edge(k2, array, t, a)

            return c

        lax.fori_loop(0, length(meta, t), body, 0)

    for t in range(tiles):

        @pl.when(t != me)
        def _():
            slab_list(own_m, 0, 0, t)

        @pl.when(slab_parity == 0)
        def _():
            slab_list(one_m, 1, 1, t)

        @pl.when(slab_parity == 1)
        def _():
            slab_list(two_m, 2, 1, t)

    scales = harmonic_scales()
    acc[...] = jnp.zeros_like(acc)
    for mine in range(nblk):
        home = mine * 4 + seat(me) * rows_dev

        def edge(e, c):
            row = edges[mine, e]
            px = data[pl.ds(home, 1), :]
            py = data[pl.ds(home + 1, 1), :]
            pz = data[pl.ds(home + 2, 1), :]
            other = jnp.concatenate([data[pl.ds(row + r, 1), :] for r in range(4)] * 2, axis=0)
            turned = other.T
            for r in range(4):
                cols[r] = jnp.broadcast_to(turned[:, r : r + 1], (128, 128))
            blk = (row % rows_dev) // 4
            dev_row = row - blk * 4 + base_meta

            def live_of(meta, off):
                return meta[dev_row - off, 2 * lists + 1 + blk].astype(jnp.int32)

            count = lax.cond(
                row < part,
                lambda: live_of(own_m, 0),
                lambda: lax.cond(row < 2 * part, lambda: live_of(one_m, part), lambda: live_of(two_m, 2 * part)),
            )

            def group(g, c2):
                for s in range(STEP):
                    at = pl.ds(pl.multiple_of((g * STEP + s) * SUB, SUB), SUB)
                    ex = cols[0, at, :] - px
                    ey = cols[1, at, :] - py
                    ez = cols[2, at, :] - pz
                    w = cols[3, at, :]
                    r2 = ex * ex + ey * ey + ez * ez
                    rs = lax.rsqrt(jnp.maximum(r2, 1e-30))
                    rho = r2 * rs
                    inv = jnp.minimum(rs, 1.0)
                    tau = rho * (1.0 / SPACING)
                    for b in range(NBIN):
                        rbuf[s, b] = jnp.maximum(0.0, 1.0 - jnp.abs(tau - (b + 1.0)))
                    for k, v in enumerate(harmonics_of(ex * inv, ey * inv, ez * inv, w)):
                        ybuf[s, k] = v
                for k in range(NHARM):
                    ys = [ybuf[s, k] for s in range(STEP)]
                    for b in range(NBIN):
                        t = ys[0] * rbuf[0, b]
                        for s in range(1, STEP):
                            t = t + ys[s] * rbuf[s, b]
                        acc[mine, k * BPAD + b] = acc[mine, k * BPAD + b] + t
                return c2

            lax.fori_loop(0, (count + STEP * SUB - 1) // (STEP * SUB), group, 0)
            return c

        lax.fori_loop(0, tally[mine], edge, 0)
        wlive = data[pl.ds(home + 3, 1), :]
        for k in range(NHARM):
            hk = jnp.sum(acc[mine, k * BPAD : (k + 1) * BPAD], axis=1) * scales[k]
            hbuf[k] = hk
            harm[mine, k * NBIN : (k + 1) * NBIN, :] = hk[:NBIN]
        for l in range(DEGREES):
            z = jnp.zeros((BPAD, BPAD), jnp.float32)
            for k in range(l * l, (l + 1) * (l + 1)):
                h = hbuf[k]
                z = z + lax.dot_general(h * wlive, h, (((1,), (1,)), ((), ())), precision=HIGH, preferred_element_type=jnp.float32)
            zeta[mine, l] = z * (1.0 / 128.0)


def shards(positions, weights, counts, pairs, pair_count):
    nblk, _, points = positions.shape
    lists = pairs.shape[1]
    tiles = lax.axis_size("tile")
    slabs = lax.axis_size("slab")
    slot = jnp.arange(points, dtype=jnp.int32)
    live = weights * (slot[None, :] < counts[:, None]).astype(jnp.float32)
    points_of = jnp.concatenate([positions, live[:, None, :]], axis=1).reshape(nblk * 4, points)
    meta = jnp.concatenate([pairs.reshape(-1), pair_count, counts]).astype(jnp.float32)
    rows_dev = -(-(nblk * 4 + 1) // 8) * 8
    packed = jnp.concatenate(
        [
            points_of,
            jnp.pad(meta, (0, points - meta.shape[0]))[None],
            jnp.zeros((rows_dev - nblk * 4 - 1, points), jnp.float32),
        ],
        axis=0,
    )
    both = ("slab", "tile")

    def move(value, hop):
        route = []
        for s in range(slabs):
            for t in range(tiles):
                s2, t2 = hop(s, t)
                if 0 <= s2 < slabs:
                    route.append((s * tiles + t, s2 * tiles + t2))
        return lax.ppermute(value, both, route)

    if tiles == 2:
        slab = jnp.concatenate([packed, move(packed, lambda s, t: (s, 1 - t))], axis=0)
    else:
        slab = lax.all_gather(packed, "tile", axis=0, tiled=True)
    near = move(slab, lambda s, t: (s + 1 - 2 * (s % 2), t))
    far = move(slab, lambda s, t: (s - 1 + 2 * (s % 2), t))
    place = jnp.stack([lax.axis_index("tile"), lax.axis_index("slab") % 2]).astype(jnp.int32)

    smem = pl.BlockSpec(memory_space=pltpu.SMEM)
    vmem = pl.BlockSpec(memory_space=pltpu.VMEM)
    body = lambda *refs: kernel(tiles, nblk, rows_dev, lists, *refs)
    harm, zeta = pl.pallas_call(
        body,
        out_shape=(
            jax.ShapeDtypeStruct((nblk, NHARM * NBIN, points), jnp.float32),
            jax.ShapeDtypeStruct((nblk, DEGREES, BPAD, BPAD), jnp.float32),
        ),
        in_specs=[smem] * 4 + [vmem] * 3,
        out_specs=(vmem, vmem),
        scratch_shapes=[
            pltpu.VMEM((3 * tiles * rows_dev, points), jnp.float32),
            pltpu.SMEM((nblk, lists * (2 * tiles + 1)), jnp.int32),
            pltpu.SMEM((nblk,), jnp.int32),
            pltpu.VMEM((4, points, points), jnp.float32),
            pltpu.VMEM((STEP, NHARM, SUB, points), jnp.float32),
            pltpu.VMEM((STEP, NBIN, SUB, points), jnp.float32),
            pltpu.VMEM((nblk, NHARM * BPAD, SUB, points), jnp.float32),
            pltpu.VMEM((NHARM, BPAD, points), jnp.float32),
        ],
    )(place, slab, near, far, slab, near, far)
    return harm, zeta[:, :, :NBIN, :NBIN].reshape(nblk, DEGREES, NBIN * NBIN)


def solution(mesh):
    return jax.shard_map(
        shards,
        mesh=mesh,
        in_specs=(
            P(("slab", "tile"), None, None),
            P(("slab", "tile"), None),
            P(("slab", "tile")),
            P(("slab", "tile"), None, None),
            P(("slab", "tile")),
        ),
        out_specs=(P(("slab", "tile"), None, None), P(("slab", "tile"), None, None)),
        check_vma=False,
    )
```

```python
import math

import jax
import jax.numpy as jnp
import numpy as np
from jax import lax
from jax.experimental import pallas as pl
from jax.experimental.pallas import tpu as pltpu
from jax.sharding import PartitionSpec as P

NBIN = 10
DEGREES = 6
NHARM = DEGREES * DEGREES
BPAD = 16
SPACING = 150.0 / (NBIN + 1)
SUB = 8
LANES = 128
COLS = NBIN * SUB
BOTH = ("slab", "tile")
f32 = jnp.float32
bf16 = jnp.bfloat16


def seat_of(l, m):
    return l * l + l + m


def legendre_sums():
    out = []
    for l in range(DEGREES):
        series = np.polynomial.legendre.leg2poly([0.0] * l + [1.0])
        for signed in range(-l, l + 1):
            m = abs(signed)
            norm = math.sqrt((2 * l + 1) / (4 * math.pi) * math.factorial(l - m) / math.factorial(l + m))
            if m > 0:
                norm *= math.sqrt(2.0)
            poly = np.polynomial.polynomial.polyder(series, m) if m else series
            out.append([(seat_of(m + a, signed), norm * float(c)) for a, c in enumerate(poly) if abs(c) > 1e-9])
    return out


def products_of(x, y, z, w):
    cosine, sine = [w], [None]
    for m in range(1, DEGREES):
        if m == 1:
            cosine.append(w * x)
            sine.append(w * y)
        else:
            cosine.append(cosine[-1] * x - sine[-1] * y)
            sine.append(sine[-1] * x + cosine[-2] * y)
    out = [None] * NHARM
    for m in range(DEGREES):
        for sign in (1, -1) if m else (1,):
            term = cosine[m] if sign > 0 else sine[m]
            for l in range(m, DEGREES):
                out[seat_of(l, sign * m)] = term
                if l < DEGREES - 1:
                    term = term * z
    return out


def halves(v):
    high = v.astype(bf16)
    return high, (v - high.astype(f32)).astype(bf16)


def stacked_halves(values):
    pairs = [halves(jnp.concatenate(values[k : k + 2], axis=0)) for k in range(0, len(values), 2)]
    return [jnp.concatenate(part, axis=0) for part in zip(*pairs)]


def operands(own, row):
    ex, ey, ez = (row[r] - own[r] for r in range(3))
    r2 = ex * ex + ey * ey + ez * ez
    rs = lax.rsqrt(jnp.maximum(r2, 1e-30))
    tau = r2 * rs
    inv = jnp.minimum(rs, SPACING)
    radial = [jnp.maximum(0.0, 1.0 - jnp.abs(tau - (b + 1.0))) for b in range(NBIN)]
    w = jnp.broadcast_to(row[3], (SUB, LANES))
    return stacked_halves(products_of(ex * inv, ey * inv, ez * inv, w)) + stacked_halves(radial)


def kernel(tiles, nblk, rows_dev, lists, *refs):
    (own_h, one_h, two_h, harm, zeta, raw, meta, sems, data, chunks, tally, wide, acc, low, hbuf) = refs
    span = tiles * nblk
    meta_row = nblk * 4
    me = lax.axis_index("tile")
    parity = lax.rem(lax.axis_index("slab"), 2)
    below = 2 - parity

    def seat(t):
        return jnp.bitwise_xor(t, me) if tiles == 2 else t

    copies = []
    for a, src in enumerate((own_h, one_h, two_h)):
        copies.append(pltpu.make_async_copy(src, raw.at[a], sems.at[len(copies)]))
        for t in range(tiles):
            line = src.at[pl.ds(t * rows_dev + meta_row, 1), :]
            copies.append(pltpu.make_async_copy(line, meta.at[pl.ds(a * tiles + t, 1), :], sems.at[len(copies)]))
    for c in copies:
        c.start()
    for k in range(nblk):
        tally[k] = 0
    for c in copies:
        c.wait()

    scale = jnp.where(lax.broadcasted_iota(jnp.int32, (4, LANES), 0) < 3, 1.0 / SPACING, 1.0)
    for a in range(3):
        for t in range(tiles):
            for k in range(nblk):
                first = t * rows_dev + k * 4
                data[(a * tiles + t) * nblk + k, 0:4, :] = raw[a, first : first + 4, :] * scale
    lane = lax.broadcasted_iota(jnp.int32, (SUB, LANES), 1)

    def number(line, at):
        return meta[line, at].astype(jnp.int32)

    def add_edge(mine, a, t, blk):
        line = a * tiles + seat(t)
        n = tally[mine]
        c, r = lax.shift_right_logical(n, 7), lax.bitwise_and(n, LANES - 1)
        turned = pltpu.roll(data[line * nblk + blk], r, axis=1)
        chunks[mine, c] = jnp.where(lane >= r, turned, chunks[mine, c])
        chunks[mine, c + 1] = jnp.where(lane < r, turned, 0.0)
        tally[mine] = n + number(line, 2 * lists + 1 + blk)

    def entry(line, p):
        a = number(line, 2 * p)
        b = number(line, 2 * p + 1)
        h = lax.div(b, span)
        rem = b - h * span
        t2 = lax.div(rem, nblk)
        return a, h, t2, rem - t2 * nblk

    own_line = seat(me)

    def own_list(p, c):
        a, h, t2, k2 = entry(own_line, p)
        add_edge(a, h * below, t2, k2)

        @pl.when((h == 0) & (t2 == me) & (k2 != a))
        def _():
            add_edge(k2, 0, me, a)

        return c

    lax.fori_loop(0, number(own_line, 2 * lists), own_list, 0)

    def neighbour(i, c):
        half = lax.div(i, tiles)
        t = i - half * tiles
        a = half * (1 + parity)
        line = a * tiles + seat(t)

        def body(p, c2):
            k, h, t2, k2 = entry(line, p)

            @pl.when((h == half) & (t2 == me))
            def _():
                add_edge(k2, a, t, k)

            return c2

        @pl.when((half == 1) | (t != me))
        def _():
            lax.fori_loop(0, number(line, 2 * lists), body, 0)

        return c

    lax.fori_loop(0, 2 * tiles, neighbour, 0)

    row_i = lax.broadcasted_iota(jnp.int32, (LANES, LANES), 0)
    col_i = lax.broadcasted_iota(jnp.int32, (LANES, LANES), 1)
    diagonal = (lax.rem(row_i, SUB) == lax.rem(col_i, SUB)) & (col_i < COLS)
    pick = (lax.div(row_i, SUB) == lax.rem(col_i, BPAD)).astype(f32).astype(bf16)
    pick = jnp.concatenate([pick, pick], axis=0)
    octet_lane = lax.div(col_i, BPAD)
    sums = legendre_sums()

    def block(mine, carry):
        home = seat(me) * nblk + mine
        turned = data[home].T
        for r in range(3):
            wide[r] = jnp.broadcast_to(turned[:, r : r + 1], (LANES, LANES))
        acc[...] = jnp.zeros_like(acc)

        def add_chunks(first, count):
            rows = [[chunks[mine, first + q, r : r + 1, :] for r in range(4)] for q in range(count)]
            blank = jnp.zeros((LANES - COLS, LANES), bf16)
            zero = jnp.zeros((COLS, LANES), bf16)
            for g in range(LANES // SUB):
                own = [wide[r, g * SUB : (g + 1) * SUB, :] for r in range(3)]
                left, right = [], []
                for q in range(count):
                    yh, yl, rh, rl = operands(own, rows[q])
                    left += [yh, yl]
                    right += [jnp.concatenate([rh, blank, rl], axis=0), jnp.concatenate([rh, blank, zero], axis=0)]
                d = lax.dot_general(
                    jnp.concatenate(left, axis=1),
                    jnp.concatenate(right, axis=1),
                    (((1,), (1,)), ((), ())),
                    preferred_element_type=f32,
                )
                acc[g, :, 0:COLS] = acc[g, :, 0:COLS] + (d[:, 0:COLS] + d[:, LANES : LANES + COLS])

        n_chunks = lax.div(tally[mine] + (LANES - 1), LANES)

        def two(i, c):
            add_chunks(2 * i, 2)
            return c

        lax.fori_loop(0, lax.div(n_chunks, 2), two, 0)

        @pl.when(lax.rem(n_chunks, 2) == 1)
        def _():
            add_chunks(n_chunks - 1, 1)

        for first in range(0, NHARM, SUB):
            flat = jnp.zeros((LANES, LANES), f32)
            for k in range(first, min(first + SUB, NHARM)):
                full = jnp.concatenate([acc[g, k * SUB : (k + 1) * SUB, :] for g in range(LANES // SUB)], axis=0)
                d = jnp.dot(
                    jnp.concatenate(halves(jnp.where(diagonal, full, 0.0)), axis=1), pick, preferred_element_type=f32
                )
                flat = jnp.where(octet_lane == k - first, d, flat)
            count = (min(first + SUB, NHARM) - first) * BPAD
            low[first * BPAD : first * BPAD + count, :] = flat.T[:count]

        w = data[home, 3:4, :]
        for k, terms in enumerate(sums):
            h = sum(low[k2 * BPAD : (k2 + 1) * BPAD, :] * c for k2, c in terms)
            hbuf[k] = h
            harm[mine, k * NBIN : (k + 1) * NBIN, :] = h[:NBIN]
        grams = []
        for l in range(DEGREES):
            left, right = [], []
            for k in range(l * l, (l + 1) * (l + 1)):
                h = hbuf[k]
                bh, bl = halves(h)
                ah, al = halves(h * w)
                left += [ah, al, ah]
                right += [bh, bh, bl]
            grams.append(
                lax.dot_general(
                    jnp.concatenate(left, axis=1),
                    jnp.concatenate(right, axis=1),
                    (((1,), (1,)), ((), ())),
                    preferred_element_type=f32,
                )
            )
        gram = jnp.concatenate(grams, axis=0) * (1.0 / LANES)
        col = lax.broadcasted_iota(jnp.int32, (BPAD, LANES), 1)
        row = lax.broadcasted_iota(jnp.int32, (BPAD, LANES), 0)
        spread = (lax.rem(col, NBIN) == row).astype(f32)
        line = jnp.dot(gram, spread, precision=lax.Precision.HIGHEST, preferred_element_type=f32)
        own_row = lax.div(col, NBIN) == row
        for l in range(DEGREES):
            got = jnp.sum(jnp.where(own_row, line[l * BPAD : (l + 1) * BPAD], 0.0), axis=0, keepdims=True)
            zeta[mine, l : l + 1, :] = got[:, : NBIN * NBIN]
        return carry

    lax.fori_loop(0, nblk, block, 0)


def shards(positions, weights, counts, pairs, pair_count):
    nblk, _, points = positions.shape
    lists = pairs.shape[1]
    tiles = lax.axis_size("tile")
    slabs = lax.axis_size("slab")
    slot = jnp.arange(points, dtype=jnp.int32)
    live = weights * (slot[None, :] < counts[:, None]).astype(f32)
    points_of = jnp.concatenate([positions, live[:, None, :]], axis=1).reshape(nblk * 4, points)
    meta = jnp.concatenate([pairs.reshape(-1), pair_count, counts]).astype(f32)
    rows_dev = -(-(nblk * 4 + 1) // 8) * 8
    packed = jnp.concatenate(
        [
            points_of,
            jnp.pad(meta, (0, points - meta.shape[0]))[None],
            jnp.zeros((rows_dev - nblk * 4 - 1, points), f32),
        ],
        axis=0,
    )

    def move(value, hop):
        route = []
        for s in range(slabs):
            for t in range(tiles):
                s2, t2 = hop(s, t)
                if 0 <= s2 < slabs:
                    route.append((s * tiles + t, s2 * tiles + t2))
        return lax.ppermute(value, BOTH, route)

    if tiles == 2:
        slab = jnp.concatenate([packed, move(packed, lambda s, t: (s, 1 - t))], axis=0)
    else:
        slab = lax.all_gather(packed, "tile", axis=0, tiled=True)
    near = move(slab, lambda s, t: (s + 1 - 2 * (s % 2), t))
    far = move(slab, lambda s, t: (s - 1 + 2 * (s % 2), t))

    anywhere = pl.BlockSpec(memory_space=pl.ANY)
    vmem = pl.BlockSpec(memory_space=pltpu.VMEM)
    deepest = lists * (2 * tiles + 1) + 2
    body = lambda *refs: kernel(tiles, nblk, rows_dev, lists, *refs)
    return pl.pallas_call(
        body,
        out_shape=(
            jax.ShapeDtypeStruct((nblk, NHARM * NBIN, points), f32),
            jax.ShapeDtypeStruct((nblk, DEGREES, NBIN * NBIN), f32),
        ),
        in_specs=[anywhere] * 3,
        out_specs=(vmem, vmem),
        scratch_shapes=[
            pltpu.VMEM((3, tiles * rows_dev, points), f32),
            pltpu.SMEM((3 * tiles, points), f32),
            pltpu.SemaphoreType.DMA((3 * (tiles + 1),)),
            pltpu.VMEM((3 * tiles * nblk, SUB, points), f32),
            pltpu.VMEM((nblk, deepest, SUB, points), f32),
            pltpu.SMEM((nblk,), jnp.int32),
            pltpu.VMEM((3, points, points), f32),
            pltpu.VMEM((points // SUB, NHARM * SUB, LANES), f32),
            pltpu.VMEM((NHARM * BPAD, points), f32),
            pltpu.VMEM((NHARM, BPAD, points), f32),
        ],
    )(slab, near, far)


def solution(mesh):
    return jax.shard_map(
        shards,
        mesh=mesh,
        in_specs=(
            P(("slab", "tile"), None, None),
            P(("slab", "tile"), None),
            P(("slab", "tile")),
            P(("slab", "tile"), None, None),
            P(("slab", "tile")),
        ),
        out_specs=(P(("slab", "tile"), None, None), P(("slab", "tile"), None, None)),
        check_vma=False,
    )
```

```python
import math

import jax
import jax.numpy as jnp
import numpy as np
from jax import lax
from jax.experimental import pallas as pl
from jax.experimental.pallas import tpu as pltpu
from jax.sharding import PartitionSpec as P

NBIN = 10
DEGREES = 6
NHARM = DEGREES * DEGREES
BPAD = 16
SPACING = 150.0 / (NBIN + 1)
SUB = 8
LANES = 128
COLS = NBIN * SUB
GROUPS = LANES // SUB
HROWS = NHARM * SUB
OCTETS = -(-NHARM // SUB)
BOTH = ("slab", "tile")
f32 = jnp.float32
bf16 = jnp.bfloat16


def seat_of(l, m):
    return l * l + l + m


def legendre_sums():
    out = []
    for l in range(DEGREES):
        series = np.polynomial.legendre.leg2poly([0.0] * l + [1.0])
        for signed in range(-l, l + 1):
            m = abs(signed)
            norm = math.sqrt((2 * l + 1) / (4 * math.pi) * math.factorial(l - m) / math.factorial(l + m))
            if m > 0:
                norm *= math.sqrt(2.0)
            poly = np.polynomial.polynomial.polyder(series, m) if m else series
            out.append([(seat_of(m + a, signed), norm * float(c)) for a, c in enumerate(poly) if abs(c) > 1e-9])
    return out


def products_of(x, y, z, w):
    cosine, sine = [w], [None]
    for m in range(1, DEGREES):
        if m == 1:
            cosine.append(w * x)
            sine.append(w * y)
        else:
            cosine.append(cosine[-1] * x - sine[-1] * y)
            sine.append(sine[-1] * x + cosine[-2] * y)
    out = [None] * NHARM
    for m in range(DEGREES):
        for sign in (1, -1) if m else (1,):
            term = cosine[m] if sign > 0 else sine[m]
            for l in range(m, DEGREES):
                out[seat_of(l, sign * m)] = term
                if l < DEGREES - 1:
                    term = term * z
    return out


def halves(v):
    high = v.astype(bf16)
    return high, (v - high.astype(f32)).astype(bf16)


def stacked_halves(values):
    pairs = [halves(jnp.concatenate(values[k : k + 2], axis=0)) for k in range(0, len(values), 2)]
    return [jnp.concatenate(part, axis=0) for part in zip(*pairs)]


def operands(own, row):
    ex, ey, ez = (row[r] - own[r] for r in range(3))
    r2 = ex * ex + ey * ey + ez * ez
    rs = lax.rsqrt(jnp.maximum(r2, 1e-30))
    tau = r2 * rs
    inv = jnp.minimum(rs, SPACING)
    radial = [jnp.maximum(0.0, 1.0 - jnp.abs(tau - (b + 1.0))) for b in range(NBIN)]
    w = jnp.broadcast_to(row[3], (SUB, LANES))
    return stacked_halves(products_of(ex * inv, ey * inv, ez * inv, w)) + stacked_halves(radial)


def kernel(tiles, nblk, rows_dev, lists, *refs):
    (own_in, one_in, two_in, harm, zeta, meta, sems, data, chunks, tally, wide, acc, low) = refs
    sources = (own_in, one_in, two_in)
    span = tiles * nblk
    meta_row = nblk * 4
    me = lax.axis_index("tile")
    parity = lax.rem(lax.axis_index("slab"), 2)
    below = 2 - parity

    def seat(t):
        return jnp.bitwise_xor(t, me) if tiles == 2 else t

    copies = []
    for a, src in enumerate(sources):
        for t in range(tiles):
            line = src.at[pl.ds(t * rows_dev + meta_row, 1), :]
            copies.append(pltpu.make_async_copy(line, meta.at[pl.ds(a * tiles + t, 1), :], sems.at[len(copies)]))
    for c in copies:
        c.start()
    for k in range(nblk):
        tally[k] = 0
    acc[...] = jnp.zeros_like(acc)

    scale = jnp.where(lax.broadcasted_iota(jnp.int32, (4, LANES), 0) < 3, 1.0 / SPACING, 1.0)
    for a in range(3):
        for t in range(tiles):
            for k in range(nblk):
                first = t * rows_dev + k * 4
                data[(a * tiles + t) * nblk + k, 0:4, :] = sources[a][first : first + 4, :] * scale
    for c in copies:
        c.wait()
    lane = lax.broadcasted_iota(jnp.int32, (SUB, LANES), 1)

    def number(line, at):
        return meta[line, at].astype(jnp.int32)

    def add_edge(mine, a, t, blk):
        line = a * tiles + seat(t)
        n = tally[mine]
        c, r = lax.shift_right_logical(n, 7), lax.bitwise_and(n, LANES - 1)
        turned = pltpu.roll(data[line * nblk + blk], r, axis=1)
        chunks[mine, c] = jnp.where(lane >= r, turned, chunks[mine, c])
        chunks[mine, c + 1] = jnp.where(lane < r, turned, 0.0)
        tally[mine] = n + number(line, 2 * lists + 1 + blk)

    def entry(line, p):
        a = number(line, 2 * p)
        b = number(line, 2 * p + 1)
        h = lax.div(b, span)
        rem = b - h * span
        t2 = lax.div(rem, nblk)
        return a, h, t2, rem - t2 * nblk

    own_line = seat(me)

    def own_list(p, c):
        a, h, t2, k2 = entry(own_line, p)
        add_edge(a, h * below, t2, k2)

        @pl.when((h == 0) & (t2 == me) & (k2 != a))
        def _():
            add_edge(k2, 0, me, a)

        return c

    lax.fori_loop(0, number(own_line, 2 * lists), own_list, 0)

    def neighbour(i, c):
        half = lax.div(i, tiles)
        t = i - half * tiles
        a = half * (1 + parity)
        line = a * tiles + seat(t)

        def body(p, c2):
            k, h, t2, k2 = entry(line, p)

            @pl.when((h == half) & (t2 == me))
            def _():
                add_edge(k2, a, t, k)

            return c2

        @pl.when((half == 1) | (t != me))
        def _():
            lax.fori_loop(0, number(line, 2 * lists), body, 0)

        return c

    lax.fori_loop(0, 2 * tiles, neighbour, 0)

    lane_block = lax.shift_right_logical(lane, 3)
    point_of = lax.bitwise_and(lane, SUB - 1)
    sums = legendre_sums()
    swaps, wanted = [], set(range(NBIN))
    for bit in (1, 2, 4, 8):
        swaps.insert(0, (bit, sorted(wanted)))
        wanted |= {x ^ bit for x in wanted}

    def block(mine, carry):
        home = seat(me) * nblk + mine
        turned = data[home].T
        for r in range(3):
            wide[r] = jnp.broadcast_to(turned[:, r : r + 1], (LANES, LANES))

        def add_chunks(first, count):
            rows = [[chunks[mine, first + q, r : r + 1, :] for r in range(4)] for q in range(count)]
            blank = jnp.zeros((LANES - COLS, LANES), bf16)
            zero = jnp.zeros((COLS, LANES), bf16)
            for g in range(GROUPS):
                own = [wide[r, g * SUB : (g + 1) * SUB, :] for r in range(3)]
                left, right = [], []
                for q in range(count):
                    yh, yl, rh, rl = operands(own, rows[q])
                    left += [yh, yl]
                    right += [jnp.concatenate([rh, blank, rl], axis=0), jnp.concatenate([rh, blank, zero], axis=0)]
                d = lax.dot_general(
                    jnp.concatenate(left, axis=1),
                    jnp.concatenate(right, axis=1),
                    (((1,), (1,)), ((), ())),
                    preferred_element_type=f32,
                )
                acc[g, 0:HROWS, 0:COLS] = acc[g, 0:HROWS, 0:COLS] + (d[:, 0:COLS] + d[:, LANES : LANES + COLS])

        n_chunks = lax.div(tally[mine] + (LANES - 1), LANES)

        def two(i, c):
            add_chunks(2 * i, 2)
            return c

        lax.fori_loop(0, lax.div(n_chunks, 2), two, 0)

        @pl.when(lax.rem(n_chunks, 2) == 1)
        def _():
            add_chunks(n_chunks - 1, 1)

        for octet in range(OCTETS):
            cur = []
            for g in range(GROUPS):
                out = None
                for i in range(SUB):
                    v = acc[g, pl.ds(octet * SUB * SUB + i, SUB, stride=SUB), :]
                    out = v if i == 0 else jnp.where(point_of == i, v, out)
                cur.append(out)
            for g in range(GROUPS):
                acc[g, octet * SUB * SUB : (octet + 1) * SUB * SUB, :] = jnp.zeros((SUB * SUB, LANES), f32)
            for bit, wanted in swaps:
                new = [None] * GROUPS
                for x in wanted:
                    if x & bit:
                        other = pltpu.roll(cur[x ^ bit], LANES - bit * SUB, axis=1)
                    else:
                        other = pltpu.roll(cur[x ^ bit], bit * SUB, axis=1)
                    new[x] = jnp.where(lax.bitwise_and(lane_block, bit) == (x & bit), cur[x], other)
                cur = new
            for b in range(NBIN):
                low[pl.ds(octet * SUB * NBIN + b, SUB, stride=NBIN), :] = cur[b]

        w = data[home, 3:4, :]
        plain = [low[k * NBIN : (k + 1) * NBIN, :] for k in range(NHARM)]
        final = [sum(plain[k2] * c for k2, c in terms) for terms in sums]
        for k, h in enumerate(final):
            harm[mine, k * NBIN : (k + 1) * NBIN, :] = h
        grams = []
        for l in range(DEGREES):
            left, right = [], []
            for k in range(l * l, (l + 1) * (l + 1)):
                h = jnp.concatenate([final[k], jnp.zeros((BPAD - NBIN, LANES), f32)], axis=0)
                bh, bl = halves(h)
                ah, al = halves(h * w)
                left += [ah, al, ah]
                right += [bh, bh, bl]
            grams.append(
                lax.dot_general(
                    jnp.concatenate(left, axis=1),
                    jnp.concatenate(right, axis=1),
                    (((1,), (1,)), ((), ())),
                    preferred_element_type=f32,
                )
            )
        gram = jnp.concatenate(grams, axis=0) * (1.0 / LANES)
        col = lax.broadcasted_iota(jnp.int32, (BPAD, LANES), 1)
        row = lax.broadcasted_iota(jnp.int32, (BPAD, LANES), 0)
        spread = (lax.rem(col, NBIN) == row).astype(f32)
        line = jnp.dot(gram, spread, precision=lax.Precision.HIGHEST, preferred_element_type=f32)
        own_row = lax.div(col, NBIN) == row
        for l in range(DEGREES):
            got = jnp.sum(jnp.where(own_row, line[l * BPAD : (l + 1) * BPAD], 0.0), axis=0, keepdims=True)
            zeta[l, pl.ds(mine, 1), :] = got[:, : NBIN * NBIN]
        return carry

    lax.fori_loop(0, nblk, block, 0)


def shards(positions, weights, counts, pairs, pair_count):
    nblk, _, points = positions.shape
    lists = pairs.shape[1]
    tiles = lax.axis_size("tile")
    slabs = lax.axis_size("slab")
    slot = jnp.arange(points, dtype=jnp.int32)
    live = weights * (slot[None, :] < counts[:, None]).astype(f32)
    points_of = jnp.concatenate([positions, live[:, None, :]], axis=1).reshape(nblk * 4, points)
    meta = jnp.concatenate([pairs.reshape(-1), pair_count, counts]).astype(f32)
    rows_dev = -(-(nblk * 4 + 1) // 8) * 8
    packed = jnp.concatenate(
        [
            points_of,
            jnp.pad(meta, (0, points - meta.shape[0]))[None],
            jnp.zeros((rows_dev - nblk * 4 - 1, points), f32),
        ],
        axis=0,
    )

    def move(value, hop):
        route = []
        for s in range(slabs):
            for t in range(tiles):
                s2, t2 = hop(s, t)
                if 0 <= s2 < slabs:
                    route.append((s * tiles + t, s2 * tiles + t2))
        return lax.ppermute(value, BOTH, route)

    if tiles == 2:
        slab = jnp.concatenate([packed, move(packed, lambda s, t: (s, 1 - t))], axis=0)
    else:
        slab = lax.all_gather(packed, "tile", axis=0, tiled=True)
    near = move(slab, lambda s, t: (s + 1 - 2 * (s % 2), t))
    far = move(slab, lambda s, t: (s - 1 + 2 * (s % 2), t))

    vmem = pl.BlockSpec(memory_space=pltpu.VMEM)
    deepest = lists * (2 * tiles + 1) + 2
    body = lambda *refs: kernel(tiles, nblk, rows_dev, lists, *refs)
    harm, zeta = pl.pallas_call(
        body,
        out_shape=(
            jax.ShapeDtypeStruct((nblk, NHARM * NBIN, points), f32),
            jax.ShapeDtypeStruct((DEGREES, nblk, NBIN * NBIN), f32),
        ),
        in_specs=[vmem] * 3,
        out_specs=(vmem, vmem),
        scratch_shapes=[
            pltpu.SMEM((3 * tiles, points), f32),
            pltpu.SemaphoreType.DMA((3 * tiles,)),
            pltpu.VMEM((3 * tiles * nblk, SUB, points), f32),
            pltpu.VMEM((nblk, deepest, SUB, points), f32),
            pltpu.SMEM((nblk,), jnp.int32),
            pltpu.VMEM((3, points, points), f32),
            pltpu.VMEM((GROUPS, OCTETS * SUB * SUB, LANES), f32),
            pltpu.VMEM((OCTETS * SUB * NBIN, points), f32),
        ],
        compiler_params=pltpu.CompilerParams(vmem_limit_bytes=24 * 1024 * 1024),
    )(slab, near, far)
    return harm, zeta.transpose(1, 0, 2)


def solution(mesh):
    return jax.shard_map(
        shards,
        mesh=mesh,
        in_specs=(
            P(("slab", "tile"), None, None),
            P(("slab", "tile"), None),
            P(("slab", "tile")),
            P(("slab", "tile"), None, None),
            P(("slab", "tile")),
        ),
        out_specs=(P(("slab", "tile"), None, None), P(("slab", "tile"), None, None)),
        check_vma=False,
    )
```

```python
import math

import jax
import jax.numpy as jnp
import numpy as np
from jax import lax
from jax.experimental import pallas as pl
from jax.experimental.pallas import tpu as pltpu
from jax.sharding import PartitionSpec as P

NBIN = 10
DEGREES = 6
NHARM = DEGREES * DEGREES
BPAD = 16
SPACING = 150.0 / (NBIN + 1)
SUB = 8
LANES = 128
COLS = NBIN * SUB
GROUPS = LANES // SUB
HROWS = NHARM * SUB
OCTETS = -(-NHARM // SUB)
BOTH = ("slab", "tile")
f32 = jnp.float32
bf16 = jnp.bfloat16


def seat_of(l, m):
    return l * l + l + m


def legendre_sums():
    out = []
    for l in range(DEGREES):
        series = np.polynomial.legendre.leg2poly([0.0] * l + [1.0])
        for signed in range(-l, l + 1):
            m = abs(signed)
            norm = math.sqrt((2 * l + 1) / (4 * math.pi) * math.factorial(l - m) / math.factorial(l + m))
            if m > 0:
                norm *= math.sqrt(2.0)
            poly = np.polynomial.polynomial.polyder(series, m) if m else series
            out.append([(seat_of(m + a, signed), norm * float(c)) for a, c in enumerate(poly) if abs(c) > 1e-9])
    return out


def products_of(x, y, z, w):
    cosine, sine = [w], [None]
    for m in range(1, DEGREES):
        if m == 1:
            cosine.append(w * x)
            sine.append(w * y)
        else:
            cosine.append(cosine[-1] * x - sine[-1] * y)
            sine.append(sine[-1] * x + cosine[-2] * y)
    out = [None] * NHARM
    for m in range(DEGREES):
        for sign in (1, -1) if m else (1,):
            term = cosine[m] if sign > 0 else sine[m]
            for l in range(m, DEGREES):
                out[seat_of(l, sign * m)] = term
                if l < DEGREES - 1:
                    term = term * z
    return out


def halves(v):
    high = v.astype(bf16)
    return high, (v - high.astype(f32)).astype(bf16)


def stacked_halves(values):
    pairs = [halves(jnp.concatenate(values[k : k + 2], axis=0)) for k in range(0, len(values), 2)]
    return [jnp.concatenate(part, axis=0) for part in zip(*pairs)]


def operands(own, row):
    ex, ey, ez = (row[r] - own[r] for r in range(3))
    r2 = ex * ex + ey * ey + ez * ez
    rs = lax.rsqrt(jnp.maximum(r2, 1e-30))
    tau = r2 * rs
    inv = jnp.minimum(rs, SPACING)
    radial = [jnp.maximum(0.0, 1.0 - jnp.abs(tau - (b + 1.0))) for b in range(NBIN)]
    w = jnp.broadcast_to(row[3], (SUB, LANES))
    return stacked_halves(products_of(ex * inv, ey * inv, ez * inv, w)) + stacked_halves(radial)


def pack_kernel(base, lists, pos, weights, pairs, counts, pair_count, out):
    nblk = weights.shape[0]
    out[...] = jnp.zeros_like(out)
    out[base : base + 2, 0:lists] = pairs[0].astype(f32)
    lane = lax.broadcasted_iota(jnp.int32, (1, LANES), 1)
    line = jnp.where(lane == 0, pair_count[0], 0)
    for k in range(nblk):
        line = jnp.where(lane == k + 1, counts[k], line)
        for r in range(3):
            out[r * nblk + k : r * nblk + k + 1, :] = pos[r, k : k + 1, :]
        out[3 * nblk + k : 3 * nblk + k + 1, :] = weights[k : k + 1, :] * (lane < counts[k]).astype(f32)
    out[base + 2 : base + 3, :] = line.astype(f32)


def kernel(tiles, nblk, rows_dev, base, lists, *refs):
    (own_in, one_in, two_in, harm, zeta, meta, sems, data, chunks, tally, wide, acc, low, grams) = refs
    sources = (own_in, one_in, two_in)
    span = tiles * nblk
    me = lax.axis_index("tile")
    parity = lax.rem(lax.axis_index("slab"), 2)
    below = 2 - parity

    def seat(t):
        return jnp.bitwise_xor(t, me) if tiles == 2 else t

    copies = []
    for a, src in enumerate(sources):
        for t in range(tiles):
            n = len(copies)
            lines = src.at[pl.ds(t * rows_dev + base, 3), :]
            copies.append(pltpu.make_async_copy(lines, meta.at[pl.ds(3 * n, 3), :], sems.at[n]))
    for c in copies:
        c.start()
    for k in range(nblk):
        tally[k] = 0
    scale = jnp.where(lax.broadcasted_iota(jnp.int32, (4, LANES), 0) < 3, 1.0 / SPACING, 1.0)
    for a in range(3):
        for t in range(tiles):
            for k in range(nblk):
                rows = sources[a][pl.ds(t * rows_dev + k, 4, stride=nblk), :]
                data[(a * tiles + t) * nblk + k, 0:4, :] = rows * scale
    for k in range(nblk):
        turned = data[seat(me) * nblk + k].T
        for r in range(3):
            wide[k, r] = jnp.broadcast_to(turned[:, r : r + 1], (LANES, LANES))
    for c in copies:
        c.wait()
    lane = lax.broadcasted_iota(jnp.int32, (SUB, LANES), 1)

    def number(line, which, at):
        return meta[3 * line + which, at].astype(jnp.int32)

    def length(line):
        return number(line, 2, 0)

    def add_edge(mine, a, t, blk):
        line = a * tiles + seat(t)
        n = tally[mine]
        c, r = lax.shift_right_logical(n, 7), lax.bitwise_and(n, LANES - 1)
        turned = pltpu.roll(data[line * nblk + blk], r, axis=1)
        chunks[mine, c] = jnp.where(lane >= r, turned, chunks[mine, c])
        chunks[mine, c + 1] = jnp.where(lane < r, turned, 0.0)
        tally[mine] = n + number(line, 2, 1 + blk)

    def entry(line, p):
        b = number(line, 1, p)
        h = lax.div(b, span)
        rem = b - h * span
        t2 = lax.div(rem, nblk)
        return number(line, 0, p), h, t2, rem - t2 * nblk

    own_line = seat(me)

    def own_list(p, c):
        a, h, t2, k2 = entry(own_line, p)
        add_edge(a, h * below, t2, k2)

        @pl.when((h == 0) & (t2 == me) & (k2 != a))
        def _():
            add_edge(k2, 0, me, a)

        return c

    lax.fori_loop(0, length(own_line), own_list, 0)

    def neighbour(i, c):
        half = lax.div(i, tiles)
        t = i - half * tiles
        a = half * (1 + parity)
        line = a * tiles + seat(t)

        def body(p, c2):
            k, h, t2, k2 = entry(line, p)

            @pl.when((h == half) & (t2 == me))
            def _():
                add_edge(k2, a, t, k)

            return c2

        @pl.when((half == 1) | (t != me))
        def _():
            lax.fori_loop(0, length(line), body, 0)

        return c

    lax.fori_loop(0, 2 * tiles, neighbour, 0)

    lane_block = lax.shift_right_logical(lane, 3)
    point_of = lax.bitwise_and(lane, SUB - 1)
    sums = legendre_sums()
    swaps, wanted = [], set(range(NBIN))
    for bit in (1, 2, 4, 8):
        swaps.insert(0, (bit, sorted(wanted)))
        wanted |= {x ^ bit for x in wanted}

    def block(mine, carry):
        home = seat(me) * nblk + mine

        def add_chunks(first, count, fresh=False):
            rows = [[chunks[mine, first + q, r : r + 1, :] for r in range(4)] for q in range(count)]
            blank = jnp.zeros((LANES - COLS, LANES), bf16)
            zero = jnp.zeros((COLS, LANES), bf16)
            for g in range(GROUPS):
                own = [wide[mine, r, g * SUB : (g + 1) * SUB, :] for r in range(3)]
                left, right = [], []
                for q in range(count):
                    yh, yl, rh, rl = operands(own, rows[q])
                    left += [yh, yl]
                    right += [jnp.concatenate([rh, blank, rl], axis=0), jnp.concatenate([rh, blank, zero], axis=0)]
                d = lax.dot_general(
                    jnp.concatenate(left, axis=1),
                    jnp.concatenate(right, axis=1),
                    (((1,), (1,)), ((), ())),
                    preferred_element_type=f32,
                )
                d = d[:, 0:COLS] + d[:, LANES : LANES + COLS]
                acc[g, 0:HROWS, 0:COLS] = d if fresh else acc[g, 0:HROWS, 0:COLS] + d

        n_chunks = lax.div(tally[mine] + (LANES - 1), LANES)

        def two(i, c):
            add_chunks(2 * i, 2)
            return c

        @pl.when(n_chunks < 2)
        def _():
            acc[...] = jnp.zeros_like(acc)

        @pl.when(n_chunks >= 2)
        def _():
            add_chunks(0, 2, fresh=True)
            lax.fori_loop(1, lax.div(n_chunks, 2), two, 0)

        @pl.when(lax.rem(n_chunks, 2) == 1)
        def _():
            add_chunks(n_chunks - 1, 1)

        w = data[home, 3:4, :]
        plain, next_l = [], 0
        for octet in range(OCTETS):
            got = min(SUB, NHARM - octet * SUB)
            cur = []
            for g in range(GROUPS):
                out = None
                for i in range(SUB):
                    v = acc[g, pl.ds(octet * SUB * SUB + i, got, stride=SUB), :]
                    out = v if i == 0 else jnp.where(point_of[:got] == i, v, out)
                if got < SUB:
                    out = jnp.concatenate([out, jnp.zeros((SUB - got, LANES), f32)], axis=0)
                cur.append(out)
            for bit, wanted in swaps:
                new = [None] * GROUPS
                for x in wanted:
                    if x & bit:
                        other = pltpu.roll(cur[x ^ bit], LANES - bit * SUB, axis=1)
                    else:
                        other = pltpu.roll(cur[x ^ bit], bit * SUB, axis=1)
                    new[x] = jnp.where(lax.bitwise_and(lane_block, bit) == (x & bit), cur[x], other)
                cur = new
            for b in range(NBIN):
                low[pl.ds(octet * SUB * NBIN + b, SUB, stride=NBIN), :] = cur[b]
            for k in range(octet * SUB, octet * SUB + got):
                plain.append(low[k * NBIN : (k + 1) * NBIN, :])
            while next_l < DEGREES and (next_l + 1) * (next_l + 1) <= len(plain):
                left, right = [], []
                for k in range(next_l * next_l, (next_l + 1) * (next_l + 1)):
                    h = sum(plain[k2] * c for k2, c in sums[k])
                    harm[mine, k * NBIN : (k + 1) * NBIN, :] = h
                    h = jnp.concatenate([h, jnp.zeros((BPAD - NBIN, LANES), f32)], axis=0)
                    bh, bl = halves(h)
                    ah, al = halves(h * w)
                    left += [ah, al, ah]
                    right += [bh, bh, bl]
                grams[mine, next_l] = lax.dot_general(
                    jnp.concatenate(left, axis=1),
                    jnp.concatenate(right, axis=1),
                    (((1,), (1,)), ((), ())),
                    preferred_element_type=f32,
                )
                next_l += 1
        return carry

    lax.fori_loop(0, nblk, block, 0)

    col = lax.broadcasted_iota(jnp.int32, (BPAD, LANES), 1)
    row = lax.broadcasted_iota(jnp.int32, (BPAD, LANES), 0)
    flat_col = (lax.rem(col, NBIN) == row).astype(f32).astype(bf16)
    flat_row = lax.div(col, NBIN) == row
    both = halves(grams[...].reshape(nblk * DEGREES * BPAD, BPAD) * (1.0 / LANES))
    line = jnp.dot(
        jnp.concatenate(both, axis=1), jnp.concatenate([flat_col, flat_col], axis=0), preferred_element_type=f32
    )
    for mine in range(nblk):
        for l in range(DEGREES):
            at = (mine * DEGREES + l) * BPAD
            flat = jnp.sum(jnp.where(flat_row, line[at : at + BPAD], 0.0), axis=0, keepdims=True)
            zeta[l, mine : mine + 1, :] = flat[:, : NBIN * NBIN]


def shards(positions, weights, counts, pairs, pair_count):
    nblk, _, points = positions.shape
    lists = pairs.shape[1]
    tiles = lax.axis_size("tile")
    slabs = lax.axis_size("slab")
    base = -(-nblk * 4 // SUB) * SUB
    rows_dev = base + SUB
    smem = pl.BlockSpec(memory_space=pltpu.SMEM)
    vmem = pl.BlockSpec(memory_space=pltpu.VMEM)
    packed = pl.pallas_call(
        lambda *refs: pack_kernel(base, lists, *refs),
        out_shape=jax.ShapeDtypeStruct((rows_dev, points), f32),
        in_specs=[vmem] * 3 + [smem] * 2,
        out_specs=vmem,
        compiler_params=pltpu.CompilerParams(vmem_limit_bytes=1024 * 1024),
    )(positions.transpose(1, 0, 2), weights, pairs.transpose(0, 2, 1), counts, pair_count)

    def move(value, hop):
        route = []
        for s in range(slabs):
            for t in range(tiles):
                s2, t2 = hop(s, t)
                if 0 <= s2 < slabs:
                    route.append((s * tiles + t, s2 * tiles + t2))
        return lax.ppermute(value, BOTH, route)

    if tiles == 2:
        slab = jnp.concatenate([packed, move(packed, lambda s, t: (s, 1 - t))], axis=0)
    else:
        slab = lax.all_gather(packed, "tile", axis=0, tiled=True)
    near = move(slab, lambda s, t: (s + 1 - 2 * (s % 2), t))
    far = move(slab, lambda s, t: (s - 1 + 2 * (s % 2), t))

    deepest = lists * (2 * tiles + 1) + 2
    body = lambda *refs: kernel(tiles, nblk, rows_dev, base, lists, *refs)
    harm, zeta = pl.pallas_call(
        body,
        out_shape=(
            jax.ShapeDtypeStruct((nblk, NHARM * NBIN, points), f32),
            jax.ShapeDtypeStruct((DEGREES, nblk, NBIN * NBIN), f32),
        ),
        in_specs=[vmem] * 3,
        out_specs=(vmem, vmem),
        scratch_shapes=[
            pltpu.SMEM((9 * tiles, points), f32),
            pltpu.SemaphoreType.DMA((3 * tiles,)),
            pltpu.VMEM((3 * tiles * nblk, SUB, points), f32),
            pltpu.VMEM((nblk, deepest, SUB, points), f32),
            pltpu.SMEM((nblk,), jnp.int32),
            pltpu.VMEM((nblk, 3, points, points), f32),
            pltpu.VMEM((GROUPS, OCTETS * SUB * SUB, LANES), f32),
            pltpu.VMEM((OCTETS * SUB * NBIN, points), f32),
            pltpu.VMEM((nblk, DEGREES, BPAD, BPAD), f32),
        ],
        compiler_params=pltpu.CompilerParams(vmem_limit_bytes=24 * 1024 * 1024),
    )(slab, near, far)
    return harm, zeta.transpose(1, 0, 2)


def solution(mesh):
    return jax.shard_map(
        shards,
        mesh=mesh,
        in_specs=(
            P(("slab", "tile"), None, None),
            P(("slab", "tile"), None),
            P(("slab", "tile")),
            P(("slab", "tile"), None, None),
            P(("slab", "tile")),
        ),
        out_specs=(P(("slab", "tile"), None, None), P(("slab", "tile"), None, None)),
        check_vma=False,
    )
```

```python
import math

import jax
import jax.numpy as jnp
import numpy as np
from jax import lax
from jax.experimental import pallas as pl
from jax.experimental.pallas import tpu as pltpu
from jax.sharding import PartitionSpec as P

NBIN = 10
DEGREES = 6
NHARM = DEGREES * DEGREES
BPAD = 16
SPACING = 150.0 / (NBIN + 1)
SUB = 8
LANES = 128
COLS = (NBIN + 1) * SUB
GROUPS = LANES // SUB
HROWS = NHARM * SUB
OCTETS = -(-NHARM // SUB)
BOTH = ("slab", "tile")
f32 = jnp.float32
bf16 = jnp.bfloat16


def seat_of(l, m):
    return l * l + l + m


def legendre_sums():
    out = []
    for l in range(DEGREES):
        series = np.polynomial.legendre.leg2poly([0.0] * l + [1.0])
        for signed in range(-l, l + 1):
            m = abs(signed)
            norm = math.sqrt((2 * l + 1) / (4 * math.pi) * math.factorial(l - m) / math.factorial(l + m))
            if m > 0:
                norm *= math.sqrt(2.0)
            poly = np.polynomial.polynomial.polyder(series, m) if m else series
            out.append([(seat_of(m + a, signed), norm * float(c)) for a, c in enumerate(poly) if abs(c) > 1e-9])
    return out


def products_of(x, y, z, w):
    cosine, sine = [w], [None]
    for m in range(1, DEGREES):
        if m == 1:
            cosine.append(w * x)
            sine.append(w * y)
        else:
            cosine.append(cosine[-1] * x - sine[-1] * y)
            sine.append(sine[-1] * x + cosine[-2] * y)
    out = [None] * NHARM
    for m in range(DEGREES):
        for sign in (1, -1) if m else (1,):
            term = cosine[m] if sign > 0 else sine[m]
            for l in range(m, DEGREES):
                out[seat_of(l, sign * m)] = term
                if l < DEGREES - 1:
                    term = term * z
    return out


def halves(v):
    high = v.astype(bf16)
    return high, (v - high.astype(f32)).astype(bf16)


def stacked_halves(values):
    pairs = [halves(jnp.concatenate(values[k : k + 2], axis=0)) for k in range(0, len(values), 2)]
    return [jnp.concatenate(part, axis=0) for part in zip(*pairs)]


def operands(own, row):
    ex, ey, ez = (row[r] - own[r] for r in range(3))
    r2 = ex * ex + ey * ey + ez * ez
    rs = lax.rsqrt(jnp.maximum(r2, 1e-30))
    tau = r2 * rs
    inv = jnp.minimum(rs, SPACING)
    gaps = [jnp.minimum(jnp.abs(tau - (b + 1.0)), 1.0) for b in range(NBIN)]
    w = jnp.broadcast_to(row[3], (SUB, LANES))
    return stacked_halves(products_of(ex * inv, ey * inv, ez * inv, w)) + stacked_halves(gaps)


def pack_kernel(base, lists, pos, weights, pairs, counts, pair_count, out):
    nblk = weights.shape[0]
    out[...] = jnp.zeros_like(out)
    out[base : base + 2, 0:lists] = pairs[0].astype(f32)
    lane = lax.broadcasted_iota(jnp.int32, (1, LANES), 1)
    numbers = counts[...].astype(f32)
    line = jnp.where(lane == 0, jnp.broadcast_to(pair_count[...].astype(f32), (1, LANES)), 0.0)
    for k in range(nblk):
        count = jnp.broadcast_to(numbers[:, k : k + 1], (1, LANES))
        line = jnp.where(lane == k + 1, count, line)
        for r in range(3):
            out[r * nblk + k : r * nblk + k + 1, :] = pos[r, k : k + 1, :]
        out[3 * nblk + k : 3 * nblk + k + 1, :] = weights[k : k + 1, :] * (lane.astype(f32) < count).astype(f32)
    out[base + 2 : base + 3, :] = line


def kernel(tiles, nblk, rows_dev, base, lists, *refs):
    (own_in, one_in, two_in, harm, zeta, meta, sems, data, chunks, tally, wide, acc, low, grams) = refs
    sources = (own_in, one_in, two_in)
    span = tiles * nblk
    me = lax.axis_index("tile")
    parity = lax.rem(lax.axis_index("slab"), 2)
    below = 2 - parity

    def seat(t):
        return jnp.bitwise_xor(t, me) if tiles == 2 else t

    copies = []
    for a, src in enumerate(sources):
        for t in range(tiles):
            n = len(copies)
            lines = src.at[pl.ds(t * rows_dev + base, 3), :]
            copies.append(pltpu.make_async_copy(lines, meta.at[pl.ds(3 * n, 3), :], sems.at[n]))
    for c in copies:
        c.start()
    for k in range(nblk):
        tally[k] = 0
    scale = jnp.where(lax.broadcasted_iota(jnp.int32, (4, LANES), 0) < 3, 1.0 / SPACING, 1.0)
    for a in range(3):
        for t in range(tiles):
            for k in range(nblk):
                rows = sources[a][pl.ds(t * rows_dev + k, 4, stride=nblk), :]
                data[(a * tiles + t) * nblk + k, 0:4, :] = rows * scale
    for k in range(nblk):
        turned = data[seat(me) * nblk + k].T
        for r in range(3):
            wide[k, r] = jnp.broadcast_to(turned[:, r : r + 1], (LANES, LANES))
    for c in copies:
        c.wait()
    lane = lax.broadcasted_iota(jnp.int32, (SUB, LANES), 1)

    def number(line, which, at):
        return meta[3 * line + which, at].astype(jnp.int32)

    def length(line):
        return number(line, 2, 0)

    def add_edge(mine, a, t, blk):
        line = a * tiles + seat(t)
        n = tally[mine]
        c, r = lax.shift_right_logical(n, 7), lax.bitwise_and(n, LANES - 1)
        turned = pltpu.roll(data[line * nblk + blk], r, axis=1)
        chunks[mine, c] = jnp.where(lane >= r, turned, chunks[mine, c])
        chunks[mine, c + 1] = jnp.where(lane < r, turned, 0.0)
        tally[mine] = n + number(line, 2, 1 + blk)

    def entry(line, p):
        b = number(line, 1, p)
        h = lax.div(b, span)
        rem = b - h * span
        t2 = lax.div(rem, nblk)
        return number(line, 0, p), h, t2, rem - t2 * nblk

    own_line = seat(me)

    def own_list(p, c):
        a, h, t2, k2 = entry(own_line, p)
        add_edge(a, h * below, t2, k2)

        @pl.when((h == 0) & (t2 == me) & (k2 != a))
        def _():
            add_edge(k2, 0, me, a)

        return c

    lax.fori_loop(0, length(own_line), own_list, 0)

    def neighbour(i, c):
        half = lax.div(i, tiles)
        t = i - half * tiles
        a = half * (1 + parity)
        line = a * tiles + seat(t)

        def body(p, c2):
            k, h, t2, k2 = entry(line, p)

            @pl.when((h == half) & (t2 == me))
            def _():
                add_edge(k2, a, t, k)

            return c2

        @pl.when((half == 1) | (t != me))
        def _():
            lax.fori_loop(0, length(line), body, 0)

        return c

    lax.fori_loop(0, 2 * tiles, neighbour, 0)

    lane_block = lax.shift_right_logical(lane, 3)
    point_of = lax.bitwise_and(lane, SUB - 1)
    sums = legendre_sums()
    swaps, wanted = [], set(range(NBIN + 1))
    for bit in (1, 2, 4, 8):
        swaps.insert(0, (bit, sorted(wanted)))
        wanted |= {x ^ bit for x in wanted}

    def block(mine, carry):
        home = seat(me) * nblk + mine

        def add_chunks(first, count, fresh=False):
            rows = [[chunks[mine, first + q, r : r + 1, :] for r in range(4)] for q in range(count)]
            ones = jnp.ones((SUB, LANES), f32)
            blank = jnp.concatenate([ones, jnp.zeros((LANES - COLS, LANES), f32)], axis=0).astype(bf16)
            zero = jnp.zeros((NBIN * SUB, LANES), bf16)
            last = jnp.zeros((2 * SUB, LANES), bf16)
            for g in range(GROUPS):
                own = [wide[mine, r, g * SUB : (g + 1) * SUB, :] for r in range(3)]
                left, right = [], []
                for q in range(count):
                    yh, yl, rh, rl = operands(own, rows[q])
                    left += [yh, yl]
                    right += [jnp.concatenate([rh, blank, rl, last], axis=0), jnp.concatenate([rh, blank, zero, last], axis=0)]
                d = lax.dot_general(
                    jnp.concatenate(left, axis=1),
                    jnp.concatenate(right, axis=1),
                    (((1,), (1,)), ((), ())),
                    preferred_element_type=f32,
                )
                d = d[:, 0:COLS] + d[:, LANES : LANES + COLS]
                acc[g, 0:HROWS, 0:COLS] = d if fresh else acc[g, 0:HROWS, 0:COLS] + d

        n_chunks = lax.div(tally[mine] + (LANES - 1), LANES)

        @pl.when(n_chunks < 2)
        def _():
            acc[...] = jnp.zeros_like(acc)

        @pl.when(n_chunks >= 2)
        def _():
            add_chunks(0, 2, fresh=True)

        start = jnp.where(n_chunks < 2, 0, 2)
        fours = lax.shift_right_logical(n_chunks - start, 2)

        def four(i, c):
            add_chunks(start + 4 * i, 4)
            return c

        lax.fori_loop(0, fours, four, 0)
        left_over = n_chunks - start - 4 * fours
        for count in range(1, 4):

            @pl.when(left_over == count)
            def _():
                add_chunks(n_chunks - count, count)

        w = data[home, 3:4, :]
        plain, next_l = [], 0
        for octet in range(OCTETS):
            got = min(SUB, NHARM - octet * SUB)
            cur = []
            for g in range(GROUPS):
                out = None
                for i in range(SUB):
                    v = acc[g, pl.ds(octet * SUB * SUB + i, got, stride=SUB), :]
                    out = v if i == 0 else jnp.where(point_of[:got] == i, v, out)
                if got < SUB:
                    out = jnp.concatenate([out, jnp.zeros((SUB - got, LANES), f32)], axis=0)
                cur.append(out)
            for bit, wanted in swaps:
                new = [None] * GROUPS
                for x in wanted:
                    if x & bit:
                        other = pltpu.roll(cur[x ^ bit], LANES - bit * SUB, axis=1)
                    else:
                        other = pltpu.roll(cur[x ^ bit], bit * SUB, axis=1)
                    new[x] = jnp.where(lax.bitwise_and(lane_block, bit) == (x & bit), cur[x], other)
                cur = new
            for b in range(NBIN):
                low[pl.ds(octet * SUB * NBIN + b, SUB, stride=NBIN), :] = cur[NBIN] - cur[b]
            for k in range(octet * SUB, octet * SUB + got):
                plain.append(low[k * NBIN : (k + 1) * NBIN, :])
            while next_l < DEGREES and (next_l + 1) * (next_l + 1) <= len(plain):
                left, right = [], []
                for k in range(next_l * next_l, (next_l + 1) * (next_l + 1)):
                    h = sum(plain[k2] * c for k2, c in sums[k])
                    harm[mine, k * NBIN : (k + 1) * NBIN, :] = h
                    h = jnp.concatenate([h, jnp.zeros((BPAD - NBIN, LANES), f32)], axis=0)
                    bh, bl = halves(h)
                    ah, al = halves(h * w)
                    left += [ah, al, ah]
                    right += [bh, bh, bl]
                grams[mine, next_l] = lax.dot_general(
                    jnp.concatenate(left, axis=1),
                    jnp.concatenate(right, axis=1),
                    (((1,), (1,)), ((), ())),
                    preferred_element_type=f32,
                )
                next_l += 1
        return carry

    lax.fori_loop(0, nblk, block, 0)

    col = lax.broadcasted_iota(jnp.int32, (BPAD, LANES), 1)
    row = lax.broadcasted_iota(jnp.int32, (BPAD, LANES), 0)
    flat_col = (lax.rem(col, NBIN) == row).astype(f32).astype(bf16)
    flat_row = lax.div(col, NBIN) == row
    both = halves(grams[...].reshape(nblk * DEGREES * BPAD, BPAD) * (1.0 / LANES))
    line = jnp.dot(
        jnp.concatenate(both, axis=1), jnp.concatenate([flat_col, flat_col], axis=0), preferred_element_type=f32
    )
    for mine in range(nblk):
        for l in range(DEGREES):
            at = (mine * DEGREES + l) * BPAD
            flat = jnp.sum(jnp.where(flat_row, line[at : at + BPAD], 0.0), axis=0, keepdims=True)
            zeta[l, mine : mine + 1, :] = flat[:, : NBIN * NBIN]


def shards(positions, weights, counts, pairs, pair_count):
    nblk, _, points = positions.shape
    lists = pairs.shape[1]
    tiles = lax.axis_size("tile")
    slabs = lax.axis_size("slab")
    base = -(-nblk * 4 // SUB) * SUB
    rows_dev = base + SUB
    vmem = pl.BlockSpec(memory_space=pltpu.VMEM)
    packed = pl.pallas_call(
        lambda *refs: pack_kernel(base, lists, *refs),
        out_shape=jax.ShapeDtypeStruct((rows_dev, points), f32),
        in_specs=[vmem] * 5,
        out_specs=vmem,
        compiler_params=pltpu.CompilerParams(vmem_limit_bytes=1024 * 1024),
    )(positions.transpose(1, 0, 2), weights, pairs.transpose(0, 2, 1), counts[None], pair_count[None])

    def move(value, hop):
        route = []
        for s in range(slabs):
            for t in range(tiles):
                s2, t2 = hop(s, t)
                if 0 <= s2 < slabs:
                    route.append((s * tiles + t, s2 * tiles + t2))
        return lax.ppermute(value, BOTH, route)

    if tiles == 2:
        slab = jnp.concatenate([packed, move(packed, lambda s, t: (s, 1 - t))], axis=0)
    else:
        slab = lax.all_gather(packed, "tile", axis=0, tiled=True)
    near = move(slab, lambda s, t: (s + 1 - 2 * (s % 2), t))
    far = move(slab, lambda s, t: (s - 1 + 2 * (s % 2), t))

    deepest = lists * (2 * tiles + 1) + 2
    body = lambda *refs: kernel(tiles, nblk, rows_dev, base, lists, *refs)
    harm, zeta = pl.pallas_call(
        body,
        out_shape=(
            jax.ShapeDtypeStruct((nblk, NHARM * NBIN, points), f32),
            jax.ShapeDtypeStruct((DEGREES, nblk, NBIN * NBIN), f32),
        ),
        in_specs=[vmem] * 3,
        out_specs=(vmem, vmem),
        scratch_shapes=[
            pltpu.SMEM((9 * tiles, points), f32),
            pltpu.SemaphoreType.DMA((3 * tiles,)),
            pltpu.VMEM((3 * tiles * nblk, SUB, points), f32),
            pltpu.VMEM((nblk, deepest, SUB, points), f32),
            pltpu.SMEM((nblk,), jnp.int32),
            pltpu.VMEM((nblk, 3, points, points), f32),
            pltpu.VMEM((GROUPS, OCTETS * SUB * SUB, LANES), f32),
            pltpu.VMEM((OCTETS * SUB * NBIN, points), f32),
            pltpu.VMEM((nblk, DEGREES, BPAD, BPAD), f32),
        ],
        compiler_params=pltpu.CompilerParams(vmem_limit_bytes=24 * 1024 * 1024),
    )(slab, near, far)
    return harm, zeta.transpose(1, 0, 2)


def solution(mesh):
    return jax.shard_map(
        shards,
        mesh=mesh,
        in_specs=(
            P(("slab", "tile"), None, None),
            P(("slab", "tile"), None),
            P(("slab", "tile")),
            P(("slab", "tile"), None, None),
            P(("slab", "tile")),
        ),
        out_specs=(P(("slab", "tile"), None, None), P(("slab", "tile"), None, None)),
        check_vma=False,
    )
```

```python
import math

import jax
import jax.numpy as jnp
import numpy as np
from jax import lax
from jax.experimental import pallas as pl
from jax.experimental.pallas import tpu as pltpu
from jax.sharding import PartitionSpec as P

NBIN = 10
DEGREES = 6
NHARM = DEGREES * DEGREES
BPAD = 16
SPACING = 150.0 / (NBIN + 1)
SUB = 8
LANES = 128
COLS = (NBIN + 1) * SUB
GROUPS = LANES // SUB
HROWS = NHARM * SUB
OCTETS = -(-NHARM // SUB)
BOTH = ("slab", "tile")
f32 = jnp.float32
bf16 = jnp.bfloat16


def seat_of(l, m):
    return l * l + l + m


def legendre_sums():
    out = []
    for l in range(DEGREES):
        series = np.polynomial.legendre.leg2poly([0.0] * l + [1.0])
        for signed in range(-l, l + 1):
            m = abs(signed)
            norm = math.sqrt((2 * l + 1) / (4 * math.pi) * math.factorial(l - m) / math.factorial(l + m))
            if m > 0:
                norm *= math.sqrt(2.0)
            poly = np.polynomial.polynomial.polyder(series, m) if m else series
            out.append([(seat_of(m + a, signed), norm * float(c)) for a, c in enumerate(poly) if abs(c) > 1e-9])
    return out


def products_of(x, y, z, w):
    cosine, sine = [w], [None]
    for m in range(1, DEGREES):
        if m == 1:
            cosine.append(w * x)
            sine.append(w * y)
        else:
            cosine.append(cosine[-1] * x - sine[-1] * y)
            sine.append(sine[-1] * x + cosine[-2] * y)
    out = [None] * NHARM
    for m in range(DEGREES):
        for sign in (1, -1) if m else (1,):
            term = cosine[m] if sign > 0 else sine[m]
            for l in range(m, DEGREES):
                out[seat_of(l, sign * m)] = term
                if l < DEGREES - 1:
                    term = term * z
    return out


def halves(v):
    high = v.astype(bf16)
    return high, (v - high.astype(f32)).astype(bf16)


def stacked_halves(values):
    pairs = [halves(jnp.concatenate(values[k : k + 2], axis=0)) for k in range(0, len(values), 2)]
    return [jnp.concatenate(part, axis=0) for part in zip(*pairs)]


def operands(own, row):
    ex, ey, ez = (row[r] - own[r] for r in range(3))
    r2 = ex * ex + ey * ey + ez * ez
    rs = lax.rsqrt(jnp.maximum(r2, 1e-30))
    tau = r2 * rs
    inv = jnp.minimum(rs, SPACING)
    gaps = [jnp.minimum(jnp.abs(tau - (b + 1.0)), 1.0) for b in range(NBIN)]
    w = jnp.broadcast_to(row[3], (SUB, LANES))
    return stacked_halves(products_of(ex * inv, ey * inv, ez * inv, w)) + stacked_halves(gaps)


def pack_kernel(base, lists, pos, weights, pairs, counts, pair_count, out):
    nblk = weights.shape[0]
    out[...] = jnp.zeros_like(out)
    out[base : base + 2, 0:lists] = pairs[0].astype(f32)
    lane = lax.broadcasted_iota(jnp.int32, (1, LANES), 1)
    numbers = counts[...].astype(f32)
    line = jnp.where(lane == 0, jnp.broadcast_to(pair_count[...].astype(f32), (1, LANES)), 0.0)
    for k in range(nblk):
        count = jnp.broadcast_to(numbers[:, k : k + 1], (1, LANES))
        line = jnp.where(lane == k + 1, count, line)
        for r in range(3):
            out[r * nblk + k : r * nblk + k + 1, :] = pos[r, k : k + 1, :]
        out[3 * nblk + k : 3 * nblk + k + 1, :] = weights[k : k + 1, :] * (lane.astype(f32) < count).astype(f32)
    out[base + 2 : base + 3, :] = line


def kernel(tiles, nblk, rows_dev, base, lists, *refs):
    (own_in, one_in, two_in, harm, zeta, meta, sems, data, chunks, tally, wide, acc, low, grams) = refs
    sources = (own_in, one_in, two_in)
    span = tiles * nblk
    me = lax.axis_index("tile")
    parity = lax.rem(lax.axis_index("slab"), 2)
    below = 2 - parity

    def seat(t):
        return jnp.bitwise_xor(t, me) if tiles == 2 else t

    copies = []
    for a, src in enumerate(sources):
        for t in range(tiles):
            n = len(copies)
            lines = src.at[pl.ds(t * rows_dev + base, 3), :]
            copies.append(pltpu.make_async_copy(lines, meta.at[pl.ds(3 * n, 3), :], sems.at[n]))
    for c in copies:
        c.start()
    for k in range(nblk):
        tally[k] = 0
    scale = jnp.where(lax.broadcasted_iota(jnp.int32, (4, LANES), 0) < 3, 1.0 / SPACING, 1.0)
    for a in range(3):
        for t in range(tiles):
            for k in range(nblk):
                rows = sources[a][pl.ds(t * rows_dev + k, 4, stride=nblk), :]
                data[(a * tiles + t) * nblk + k, 0:4, :] = rows * scale
    for k in range(nblk):
        turned = data[seat(me) * nblk + k].T
        for r in range(3):
            wide[k, r] = jnp.broadcast_to(turned[:, r : r + 1], (LANES, LANES))
    for c in copies:
        c.wait()
    lane = lax.broadcasted_iota(jnp.int32, (SUB, LANES), 1)

    def number(line, which, at):
        return meta[3 * line + which, at].astype(jnp.int32)

    def length(line):
        return number(line, 2, 0)

    def add_edge(mine, a, t, blk):
        line = a * tiles + seat(t)
        n = tally[mine]
        c, r = lax.shift_right_logical(n, 7), lax.bitwise_and(n, LANES - 1)
        turned = pltpu.roll(data[line * nblk + blk], r, axis=1)
        chunks[mine, c] = jnp.where(lane >= r, turned, chunks[mine, c])
        chunks[mine, c + 1] = jnp.where(lane < r, turned, 0.0)
        tally[mine] = n + number(line, 2, 1 + blk)

    def entry(line, p):
        b = number(line, 1, p)
        h = lax.div(b, span)
        rem = b - h * span
        t2 = lax.div(rem, nblk)
        return number(line, 0, p), h, t2, rem - t2 * nblk

    own_line = seat(me)

    def own_list(p, c):
        a, h, t2, k2 = entry(own_line, p)
        add_edge(a, h * below, t2, k2)

        @pl.when((h == 0) & (t2 == me) & (k2 != a))
        def _():
            add_edge(k2, 0, me, a)

        return c

    lax.fori_loop(0, length(own_line), own_list, 0)

    def neighbour(i, c):
        half = lax.div(i, tiles)
        t = i - half * tiles
        a = half * (1 + parity)
        line = a * tiles + seat(t)

        def body(p, c2):
            k, h, t2, k2 = entry(line, p)

            @pl.when((h == half) & (t2 == me))
            def _():
                add_edge(k2, a, t, k)

            return c2

        @pl.when((half == 1) | (t != me))
        def _():
            lax.fori_loop(0, length(line), body, 0)

        return c

    lax.fori_loop(0, 2 * tiles, neighbour, 0)

    lane_block = lax.shift_right_logical(lane, 3)
    point_of = lax.bitwise_and(lane, SUB - 1)
    sums = legendre_sums()
    swaps, wanted = [], set(range(NBIN + 1))
    for bit in (1, 2, 4, 8):
        swaps.insert(0, (bit, sorted(wanted)))
        wanted |= {x ^ bit for x in wanted}

    def block(mine, carry):
        home = seat(me) * nblk + mine

        def add_chunks(first, count, fresh=False):
            rows = [[chunks[mine, first + q, r : r + 1, :] for r in range(4)] for q in range(count)]
            ones = jnp.ones((SUB, LANES), f32)
            blank = jnp.concatenate([ones, jnp.zeros((LANES - COLS, LANES), f32)], axis=0).astype(bf16)
            zero = jnp.zeros((NBIN * SUB, LANES), bf16)
            last = jnp.zeros((2 * SUB, LANES), bf16)
            for g in range(GROUPS):
                own = [wide[mine, r, g * SUB : (g + 1) * SUB, :] for r in range(3)]
                left, right = [], []
                for q in range(count):
                    yh, yl, rh, rl = operands(own, rows[q])
                    left += [yh, yl]
                    right += [jnp.concatenate([rh, blank, rl, last], axis=0), jnp.concatenate([rh, blank, zero, last], axis=0)]
                d = lax.dot_general(
                    jnp.concatenate(left, axis=1),
                    jnp.concatenate(right, axis=1),
                    (((1,), (1,)), ((), ())),
                    preferred_element_type=f32,
                )
                d = d[:, 0:COLS] + d[:, LANES : LANES + COLS]
                acc[g, 0:HROWS, 0:COLS] = d if fresh else acc[g, 0:HROWS, 0:COLS] + d

        n_chunks = lax.div(tally[mine] + (LANES - 1), LANES)

        lead = jnp.where(n_chunks <= 4, n_chunks, jnp.where(lax.bitwise_and(n_chunks, 3) == 1, 2, 4))

        @pl.when(lead == 0)
        def _():
            acc[...] = jnp.zeros_like(acc)

        for count in range(1, 5):

            @pl.when(lead == count)
            def _():
                add_chunks(0, count, fresh=True)

        fours = lax.shift_right_logical(n_chunks - lead, 2)

        def four(i, c):
            add_chunks(lead + 4 * i, 4)
            return c

        lax.fori_loop(0, fours, four, 0)
        left_over = n_chunks - lead - 4 * fours
        for count in (2, 3):

            @pl.when(left_over == count)
            def _():
                add_chunks(n_chunks - count, count)

        w = data[home, 3:4, :]
        plain, next_l = [], 0
        for octet in range(OCTETS):
            got = min(SUB, NHARM - octet * SUB)
            cur = []
            for g in range(GROUPS):
                out = None
                for i in range(SUB):
                    v = acc[g, pl.ds(octet * SUB * SUB + i, got, stride=SUB), :]
                    out = v if i == 0 else jnp.where(point_of[:got] == i, v, out)
                if got < SUB:
                    out = jnp.concatenate([out, jnp.zeros((SUB - got, LANES), f32)], axis=0)
                cur.append(out)
            for bit, wanted in swaps:
                new = [None] * GROUPS
                for x in wanted:
                    if x & bit:
                        other = pltpu.roll(cur[x ^ bit], LANES - bit * SUB, axis=1)
                    else:
                        other = pltpu.roll(cur[x ^ bit], bit * SUB, axis=1)
                    new[x] = jnp.where(lax.bitwise_and(lane_block, bit) == (x & bit), cur[x], other)
                cur = new
            for b in range(NBIN):
                low[pl.ds(octet * SUB * NBIN + b, SUB, stride=NBIN), :] = cur[NBIN] - cur[b]
            for k in range(octet * SUB, octet * SUB + got):
                plain.append(low[k * NBIN : (k + 1) * NBIN, :])
            while next_l < DEGREES and (next_l + 1) * (next_l + 1) <= len(plain):
                left, right = [], []
                for k in range(next_l * next_l, (next_l + 1) * (next_l + 1)):
                    h = sum(plain[k2] * c for k2, c in sums[k])
                    harm[mine, k * NBIN : (k + 1) * NBIN, :] = h
                    h = jnp.concatenate([h, jnp.zeros((BPAD - NBIN, LANES), f32)], axis=0)
                    bh, bl = halves(h)
                    ah, al = halves(h * w)
                    left += [ah, al, ah]
                    right += [bh, bh, bl]
                grams[mine, next_l] = lax.dot_general(
                    jnp.concatenate(left, axis=1),
                    jnp.concatenate(right, axis=1),
                    (((1,), (1,)), ((), ())),
                    preferred_element_type=f32,
                )
                next_l += 1
        return carry

    lax.fori_loop(0, nblk, block, 0)

    col = lax.broadcasted_iota(jnp.int32, (BPAD, LANES), 1)
    row = lax.broadcasted_iota(jnp.int32, (BPAD, LANES), 0)
    flat_col = (lax.rem(col, NBIN) == row).astype(f32).astype(bf16)
    flat_row = lax.div(col, NBIN) == row
    both = halves(grams[...].reshape(nblk * DEGREES * BPAD, BPAD) * (1.0 / LANES))
    line = jnp.dot(
        jnp.concatenate(both, axis=1), jnp.concatenate([flat_col, flat_col], axis=0), preferred_element_type=f32
    )
    for mine in range(nblk):
        for l in range(DEGREES):
            at = (mine * DEGREES + l) * BPAD
            flat = jnp.sum(jnp.where(flat_row, line[at : at + BPAD], 0.0), axis=0, keepdims=True)
            zeta[l, mine : mine + 1, :] = flat[:, : NBIN * NBIN]


def shards(positions, weights, counts, pairs, pair_count):
    nblk, _, points = positions.shape
    lists = pairs.shape[1]
    tiles = lax.axis_size("tile")
    slabs = lax.axis_size("slab")
    base = -(-nblk * 4 // SUB) * SUB
    rows_dev = base + SUB
    vmem = pl.BlockSpec(memory_space=pltpu.VMEM)
    packed = pl.pallas_call(
        lambda *refs: pack_kernel(base, lists, *refs),
        out_shape=jax.ShapeDtypeStruct((rows_dev, points), f32),
        in_specs=[vmem] * 5,
        out_specs=vmem,
        compiler_params=pltpu.CompilerParams(vmem_limit_bytes=1024 * 1024),
    )(positions.transpose(1, 0, 2), weights, pairs.transpose(0, 2, 1), counts[None], pair_count[None])

    def move(value, hop):
        route = []
        for s in range(slabs):
            for t in range(tiles):
                s2, t2 = hop(s, t)
                if 0 <= s2 < slabs:
                    route.append((s * tiles + t, s2 * tiles + t2))
        return lax.ppermute(value, BOTH, route)

    if tiles == 2:
        slab = jnp.concatenate([packed, move(packed, lambda s, t: (s, 1 - t))], axis=0)
    else:
        slab = lax.all_gather(packed, "tile", axis=0, tiled=True)
    near = move(slab, lambda s, t: (s + 1 - 2 * (s % 2), t))
    far = move(slab, lambda s, t: (s - 1 + 2 * (s % 2), t))

    deepest = lists * (2 * tiles + 1) + 2
    body = lambda *refs: kernel(tiles, nblk, rows_dev, base, lists, *refs)
    harm, zeta = pl.pallas_call(
        body,
        out_shape=(
            jax.ShapeDtypeStruct((nblk, NHARM * NBIN, points), f32),
            jax.ShapeDtypeStruct((DEGREES, nblk, NBIN * NBIN), f32),
        ),
        in_specs=[vmem] * 3,
        out_specs=(vmem, vmem),
        scratch_shapes=[
            pltpu.SMEM((9 * tiles, points), f32),
            pltpu.SemaphoreType.DMA((3 * tiles,)),
            pltpu.VMEM((3 * tiles * nblk, SUB, points), f32),
            pltpu.VMEM((nblk, deepest, SUB, points), f32),
            pltpu.SMEM((nblk,), jnp.int32),
            pltpu.VMEM((nblk, 3, points, points), f32),
            pltpu.VMEM((GROUPS, OCTETS * SUB * SUB, LANES), f32),
            pltpu.VMEM((OCTETS * SUB * NBIN, points), f32),
            pltpu.VMEM((nblk, DEGREES, BPAD, BPAD), f32),
        ],
        compiler_params=pltpu.CompilerParams(vmem_limit_bytes=24 * 1024 * 1024),
    )(slab, near, far)
    return harm, zeta.transpose(1, 0, 2)


def solution(mesh):
    return jax.shard_map(
        shards,
        mesh=mesh,
        in_specs=(
            P(("slab", "tile"), None, None),
            P(("slab", "tile"), None),
            P(("slab", "tile")),
            P(("slab", "tile"), None, None),
            P(("slab", "tile")),
        ),
        out_specs=(P(("slab", "tile"), None, None), P(("slab", "tile"), None, None)),
        check_vma=False,
    )
```

```python
import math

import jax
import jax.numpy as jnp
import numpy as np
from jax import lax
from jax.experimental import pallas as pl
from jax.experimental.pallas import tpu as pltpu
from jax.sharding import PartitionSpec as P

NBIN = 10
DEGREES = 6
NHARM = DEGREES * DEGREES
BPAD = 16
SPACING = 150.0 / (NBIN + 1)
SUB = 8
LANES = 128
COLS = (NBIN + 1) * SUB
GROUPS = LANES // SUB
HROWS = NHARM * SUB
OCTETS = -(-NHARM // SUB)
BOTH = ("slab", "tile")
f32 = jnp.float32
bf16 = jnp.bfloat16


def seat_of(l, m):
    return l * l + l + m


def legendre_sums():
    out = []
    for l in range(DEGREES):
        series = np.polynomial.legendre.leg2poly([0.0] * l + [1.0])
        for signed in range(-l, l + 1):
            m = abs(signed)
            norm = math.sqrt((2 * l + 1) / (4 * math.pi) * math.factorial(l - m) / math.factorial(l + m))
            if m > 0:
                norm *= math.sqrt(2.0)
            poly = np.polynomial.polynomial.polyder(series, m) if m else series
            out.append([(seat_of(m + a, signed), norm * float(c)) for a, c in enumerate(poly) if abs(c) > 1e-9])
    return out


def products_of(x, y, z, w):
    cosine, sine = [w], [None]
    for m in range(1, DEGREES):
        if m == 1:
            cosine.append(w * x)
            sine.append(w * y)
        else:
            cosine.append(cosine[-1] * x - sine[-1] * y)
            sine.append(sine[-1] * x + cosine[-2] * y)
    out = [None] * NHARM
    for m in range(DEGREES):
        for sign in (1, -1) if m else (1,):
            term = cosine[m] if sign > 0 else sine[m]
            for l in range(m, DEGREES):
                out[seat_of(l, sign * m)] = term
                if l < DEGREES - 1:
                    term = term * z
    return out


def halves(v):
    high = v.astype(bf16)
    return high, (v - high.astype(f32)).astype(bf16)


def stacked_halves(values):
    pairs = [halves(jnp.concatenate(values[k : k + 2], axis=0)) for k in range(0, len(values), 2)]
    return [jnp.concatenate(part, axis=0) for part in zip(*pairs)]


def operands(own, row):
    ex, ey, ez = (row[r] - own[r] for r in range(3))
    r2 = ex * ex + ey * ey + ez * ez
    rs = lax.rsqrt(jnp.maximum(r2, 1e-30))
    tau = r2 * rs
    inv = jnp.minimum(rs, SPACING)
    gaps = [jnp.minimum(jnp.abs(tau - (b + 1.0)), 1.0) for b in range(NBIN)]
    w = jnp.broadcast_to(row[3], (SUB, LANES))
    return stacked_halves(products_of(ex * inv, ey * inv, ez * inv, w)) + stacked_halves(gaps)


def pack_kernel(base, lists, pos, weights, pairs, counts, pair_count, out):
    nblk = weights.shape[0]
    out[...] = jnp.zeros_like(out)
    lane = lax.broadcasted_iota(jnp.int32, (1, LANES), 1)
    numbers = counts[...].astype(f32)
    line = jnp.where(lane == 2 * lists, jnp.broadcast_to(pair_count[...].astype(f32), (1, LANES)), 0.0)
    for k in range(nblk):
        count = jnp.broadcast_to(numbers[:, k : k + 1], (1, LANES))
        line = jnp.where(lane == 2 * lists + 1 + k, count, line)
        for r in range(3):
            out[r * nblk + k : r * nblk + k + 1, :] = pos[r, k : k + 1, :]
        out[3 * nblk + k : 3 * nblk + k + 1, :] = weights[k : k + 1, :] * (lane.astype(f32) < count).astype(f32)
    out[base : base + 1, :] = line
    for half in range(2):
        out[base : base + 1, half * lists : (half + 1) * lists] = pairs[0, half : half + 1, :].astype(f32)


def kernel(tiles, nblk, rows_dev, base, lists, *refs):
    (own_in, one_in, two_in, harm, zeta, meta, sems, data, chunks, tally, wide, acc, low, grams) = refs
    sources = (own_in, one_in, two_in)
    span = tiles * nblk
    me = lax.axis_index("tile")
    parity = lax.rem(lax.axis_index("slab"), 2)
    below = 2 - parity

    def seat(t):
        return jnp.bitwise_xor(t, me) if tiles == 2 else t

    copies = []
    for a, src in enumerate(sources):
        for t in range(tiles):
            n = len(copies)
            lines = src.at[pl.ds(t * rows_dev + base, 1), :]
            copies.append(pltpu.make_async_copy(lines, meta.at[pl.ds(n, 1), :], sems.at[n]))
    for c in copies:
        c.start()
    for k in range(nblk):
        tally[k] = 0
    scale = jnp.where(lax.broadcasted_iota(jnp.int32, (4, LANES), 0) < 3, 1.0 / SPACING, 1.0)
    for a in range(3):
        for t in range(tiles):
            for k in range(nblk):
                rows = sources[a][pl.ds(t * rows_dev + k, 4, stride=nblk), :]
                data[(a * tiles + t) * nblk + k, 0:4, :] = rows * scale
    for k in range(nblk):
        turned = data[seat(me) * nblk + k].T
        for r in range(3):
            wide[k, r] = jnp.broadcast_to(turned[:, r : r + 1], (LANES, LANES))
    for c in copies:
        c.wait()
    lane = lax.broadcasted_iota(jnp.int32, (SUB, LANES), 1)

    def number(line, which, at):
        return meta[line, which * lists + at].astype(jnp.int32)

    def length(line):
        return number(line, 2, 0)

    def add_edge(mine, a, t, blk):
        line = a * tiles + seat(t)
        n = tally[mine]
        c, r = lax.shift_right_logical(n, 7), lax.bitwise_and(n, LANES - 1)
        turned = pltpu.roll(data[line * nblk + blk], r, axis=1)
        chunks[mine, c] = jnp.where(lane >= r, turned, chunks[mine, c])
        chunks[mine, c + 1] = jnp.where(lane < r, turned, 0.0)
        tally[mine] = n + number(line, 2, 1 + blk)

    def entry(line, p):
        b = number(line, 1, p)
        h = lax.div(b, span)
        rem = b - h * span
        t2 = lax.div(rem, nblk)
        return number(line, 0, p), h, t2, rem - t2 * nblk

    own_line = seat(me)

    def own_list(p, c):
        a, h, t2, k2 = entry(own_line, p)
        add_edge(a, h * below, t2, k2)

        @pl.when((h == 0) & (t2 == me) & (k2 != a))
        def _():
            add_edge(k2, 0, me, a)

        return c

    lax.fori_loop(0, length(own_line), own_list, 0)

    def neighbour(i, c):
        half = lax.div(i, tiles)
        t = i - half * tiles
        a = half * (1 + parity)
        line = a * tiles + seat(t)

        def body(p, c2):
            k, h, t2, k2 = entry(line, p)

            @pl.when((h == half) & (t2 == me))
            def _():
                add_edge(k2, a, t, k)

            return c2

        @pl.when((half == 1) | (t != me))
        def _():
            lax.fori_loop(0, length(line), body, 0)

        return c

    lax.fori_loop(0, 2 * tiles, neighbour, 0)

    lane_block = lax.shift_right_logical(lane, 3)
    point_of = lax.bitwise_and(lane, SUB - 1)
    sums = legendre_sums()
    swaps, wanted = [], set(range(NBIN + 1))
    for bit in (1, 2, 4, 8):
        swaps.insert(0, (bit, sorted(wanted)))
        wanted |= {x ^ bit for x in wanted}

    def block(mine, carry):
        home = seat(me) * nblk + mine

        def add_chunks(first, count, fresh=False):
            rows = [[chunks[mine, first + q, r : r + 1, :] for r in range(4)] for q in range(count)]
            ones = jnp.ones((SUB, LANES), f32)
            blank = jnp.concatenate([ones, jnp.zeros((LANES - COLS, LANES), f32)], axis=0).astype(bf16)
            zero = jnp.zeros((NBIN * SUB, LANES), bf16)
            last = jnp.zeros((2 * SUB, LANES), bf16)
            for g in range(GROUPS):
                own = [wide[mine, r, g * SUB : (g + 1) * SUB, :] for r in range(3)]
                left, right = [], []
                for q in range(count):
                    yh, yl, rh, rl = operands(own, rows[q])
                    left += [yh, yl]
                    right += [jnp.concatenate([rh, blank, rl, last], axis=0), jnp.concatenate([rh, blank, zero, last], axis=0)]
                d = lax.dot_general(
                    jnp.concatenate(left, axis=1),
                    jnp.concatenate(right, axis=1),
                    (((1,), (1,)), ((), ())),
                    preferred_element_type=f32,
                )
                d = d[:, 0:COLS] + d[:, LANES : LANES + COLS]
                acc[g, 0:HROWS, 0:COLS] = d if fresh else acc[g, 0:HROWS, 0:COLS] + d

        n_chunks = lax.div(tally[mine] + (LANES - 1), LANES)

        lead = jnp.where(n_chunks <= 4, n_chunks, jnp.where(lax.bitwise_and(n_chunks, 3) == 1, 2, 4))

        @pl.when(lead == 0)
        def _():
            acc[...] = jnp.zeros_like(acc)

        for count in range(1, 5):

            @pl.when(lead == count)
            def _():
                add_chunks(0, count, fresh=True)

        fours = lax.shift_right_logical(n_chunks - lead, 2)

        def four(i, c):
            add_chunks(lead + 4 * i, 4)
            return c

        lax.fori_loop(0, fours, four, 0)
        left_over = n_chunks - lead - 4 * fours
        for count in (2, 3):

            @pl.when(left_over == count)
            def _():
                add_chunks(n_chunks - count, count)

        w = data[home, 3:4, :]
        plain, next_l = [], 0
        for octet in range(OCTETS):
            got = min(SUB, NHARM - octet * SUB)
            cur = []
            for g in range(GROUPS):
                out = None
                for i in range(SUB):
                    v = acc[g, pl.ds(octet * SUB * SUB + i, got, stride=SUB), :]
                    out = v if i == 0 else jnp.where(point_of[:got] == i, v, out)
                if got < SUB:
                    out = jnp.concatenate([out, jnp.zeros((SUB - got, LANES), f32)], axis=0)
                cur.append(out)
            for bit, wanted in swaps:
                new = [None] * GROUPS
                for x in wanted:
                    if x & bit:
                        other = pltpu.roll(cur[x ^ bit], LANES - bit * SUB, axis=1)
                    else:
                        other = pltpu.roll(cur[x ^ bit], bit * SUB, axis=1)
                    new[x] = jnp.where(lax.bitwise_and(lane_block, bit) == (x & bit), cur[x], other)
                cur = new
            for b in range(NBIN):
                low[pl.ds(octet * SUB * NBIN + b, SUB, stride=NBIN), :] = cur[NBIN] - cur[b]
            for k in range(octet * SUB, octet * SUB + got):
                plain.append(low[k * NBIN : (k + 1) * NBIN, :])
            while next_l < DEGREES and (next_l + 1) * (next_l + 1) <= len(plain):
                left, right = [], []
                for k in range(next_l * next_l, (next_l + 1) * (next_l + 1)):
                    h = sum(plain[k2] * c for k2, c in sums[k])
                    harm[mine, k * NBIN : (k + 1) * NBIN, :] = h
                    h = jnp.concatenate([h, jnp.zeros((BPAD - NBIN, LANES), f32)], axis=0)
                    bh, bl = halves(h)
                    ah, al = halves(h * w)
                    left += [ah, al, ah]
                    right += [bh, bh, bl]
                grams[mine, next_l] = lax.dot_general(
                    jnp.concatenate(left, axis=1),
                    jnp.concatenate(right, axis=1),
                    (((1,), (1,)), ((), ())),
                    preferred_element_type=f32,
                )
                next_l += 1
        return carry

    lax.fori_loop(0, nblk, block, 0)

    col = lax.broadcasted_iota(jnp.int32, (BPAD, LANES), 1)
    row = lax.broadcasted_iota(jnp.int32, (BPAD, LANES), 0)
    flat_col = (lax.rem(col, NBIN) == row).astype(f32).astype(bf16)
    flat_row = lax.div(col, NBIN) == row
    both = halves(grams[...].reshape(nblk * DEGREES * BPAD, BPAD) * (1.0 / LANES))
    line = jnp.dot(
        jnp.concatenate(both, axis=1), jnp.concatenate([flat_col, flat_col], axis=0), preferred_element_type=f32
    )
    for mine in range(nblk):
        for l in range(DEGREES):
            at = (mine * DEGREES + l) * BPAD
            flat = jnp.sum(jnp.where(flat_row, line[at : at + BPAD], 0.0), axis=0, keepdims=True)
            zeta[l, mine : mine + 1, :] = flat[:, : NBIN * NBIN]


def shards(positions, weights, counts, pairs, pair_count):
    nblk, _, points = positions.shape
    lists = pairs.shape[1]
    tiles = lax.axis_size("tile")
    slabs = lax.axis_size("slab")
    base = -(-nblk * 4 // SUB) * SUB
    rows_dev = base + SUB
    vmem = pl.BlockSpec(memory_space=pltpu.VMEM)
    packed = pl.pallas_call(
        lambda *refs: pack_kernel(base, lists, *refs),
        out_shape=jax.ShapeDtypeStruct((rows_dev, points), f32),
        in_specs=[vmem] * 5,
        out_specs=vmem,
        compiler_params=pltpu.CompilerParams(vmem_limit_bytes=1024 * 1024),
    )(positions.transpose(1, 0, 2), weights, pairs.transpose(0, 2, 1), counts[None], pair_count[None])

    def move(value, hop):
        route = []
        for s in range(slabs):
            for t in range(tiles):
                s2, t2 = hop(s, t)
                if 0 <= s2 < slabs:
                    route.append((s * tiles + t, s2 * tiles + t2))
        return lax.ppermute(value, BOTH, route)

    if tiles == 2:
        slab = jnp.concatenate([packed, move(packed, lambda s, t: (s, 1 - t))], axis=0)
    else:
        slab = lax.all_gather(packed, "tile", axis=0, tiled=True)
    near = move(slab, lambda s, t: (s + 1 - 2 * (s % 2), t))
    far = move(slab, lambda s, t: (s - 1 + 2 * (s % 2), t))

    deepest = lists * (2 * tiles + 1) + 2
    body = lambda *refs: kernel(tiles, nblk, rows_dev, base, lists, *refs)
    harm, zeta = pl.pallas_call(
        body,
        out_shape=(
            jax.ShapeDtypeStruct((nblk, NHARM * NBIN, points), f32),
            jax.ShapeDtypeStruct((DEGREES, nblk, NBIN * NBIN), f32),
        ),
        in_specs=[vmem] * 3,
        out_specs=(vmem, vmem),
        scratch_shapes=[
            pltpu.SMEM((3 * tiles, points), f32),
            pltpu.SemaphoreType.DMA((3 * tiles,)),
            pltpu.VMEM((3 * tiles * nblk, SUB, points), f32),
            pltpu.VMEM((nblk, deepest, SUB, points), f32),
            pltpu.SMEM((nblk,), jnp.int32),
            pltpu.VMEM((nblk, 3, points, points), f32),
            pltpu.VMEM((GROUPS, OCTETS * SUB * SUB, LANES), f32),
            pltpu.VMEM((OCTETS * SUB * NBIN, points), f32),
            pltpu.VMEM((nblk, DEGREES, BPAD, BPAD), f32),
        ],
        compiler_params=pltpu.CompilerParams(vmem_limit_bytes=24 * 1024 * 1024),
    )(slab, near, far)
    return harm, zeta.transpose(1, 0, 2)


def solution(mesh):
    return jax.shard_map(
        shards,
        mesh=mesh,
        in_specs=(
            P(("slab", "tile"), None, None),
            P(("slab", "tile"), None),
            P(("slab", "tile")),
            P(("slab", "tile"), None, None),
            P(("slab", "tile")),
        ),
        out_specs=(P(("slab", "tile"), None, None), P(("slab", "tile"), None, None)),
        check_vma=False,
    )
```
